1024 devices in a mesh: fsdp: 16 (over z), tensor: 64 (over y, x, core).
Axes of the slice: x: 4, y: 8, z: 16, core: 2. Of those that a mesh axis runs over, the one named last changes fastest.
Arguments:
- momentum: float32 [16, 1152, 7168], P(None, 'fsdp', 'tensor'), may hold values from -600 to 600
- gradient: float32 [16, 1152, 7168], P(None, 'fsdp', 'tensor'), may hold values from -600 to 600
- live_ranks: int32 [16], replicated, may hold values from 0 to 1, as said below
- owner_group: int32 [16], replicated, may hold values from 0 to 15, each once
- row_counts: int32 [16, 16], replicated, may hold values from 1 to 72, as said below
- row_offsets: int32 [16, 16], replicated, may hold values from 0 to 575, as said below
Outputs:
- new_momentum: float32 [16, 1152, 7168], P(None, 'fsdp', 'tensor')
- update_shards: float32 [16, 1152, 7168], P(None, 'fsdp', 'tensor')
- owned_update: float32 [16, 576, 7168], P('fsdp', None, 'tensor')
The draws below stay inside these ranges and needn't reach their ends.
Inputs may be any that keep to these rules, and one draw needn't show every extreme that they name: `live_ranks`: exactly one rank is dead. For every matrix the live ranks' segments [row_offsets, row_offsets + row_counts) are disjoint and cover all 576 rows, and one live rank holds exactly 72 rows. The dead rank's entries are stale and describe no rows. `row_offsets`: see row_counts.
All inputs are finite; a program needn't handle non-finite values.
Results may differ from the reference program's by a relative error of at most 0.0003.
Values sent between devices are 32-bit elements; how exact they have to be, the bound alone decides.
A program may use at most 32 MiB of HBM per device.

```python
import math
import jax
import jax.numpy as jnp
from jax import lax

WIDTH = 7168
INNER = 576
ITERS = 2
MATS = 16
CAP = 72
SLOTS = 1152
N_FSDP = 16


def scaled_field(key, salt):
    key_main = jax.random.fold_in(key, salt)
    key_entries, key_rows, key_columns = jax.random.split(key_main, 3)
    entries = jax.random.truncated_normal(key_entries, -5.0, 5.0, (MATS, SLOTS, WIDTH), jnp.float32)
    spread = math.log(10.0)
    row_scale = jnp.exp(jax.random.uniform(key_rows, (MATS, SLOTS, 1), jnp.float32, 0.0, spread))
    column_scale = jnp.exp(jax.random.uniform(key_columns, (MATS, 1, WIDTH), jnp.float32, 0.0, spread))
    return entries * row_scale * column_scale


def rank_order(sub_key):
    return jax.random.permutation(sub_key, N_FSDP).astype(jnp.int32)


def layout_tables(key):
    key_main = jax.random.fold_in(key, 9173)
    key_dead, key_order, key_shift, key_stale, key_start = jax.random.split(key_main, 5)
    rank_ids = jnp.arange(N_FSDP, dtype=jnp.int32)
    first_matrix = (jnp.arange(MATS, dtype=jnp.int32) == 0)[:, None]
    dead_rank = jax.random.randint(key_dead, (), 0, N_FSDP, dtype=jnp.int32)
    alive_flags = (rank_ids != dead_rank).astype(jnp.int32)
    orders = jax.vmap(rank_order)(jax.random.split(key_order, MATS))
    matches = (orders[:, :, None] == rank_ids[None, None, :]).astype(jnp.int32)
    placing = jnp.sum(matches * rank_ids[None, :, None], axis=1)
    is_dead = (rank_ids == dead_rank)[None, :]
    dead_place = jnp.sum(placing * is_dead.astype(jnp.int32), axis=1, keepdims=True)
    live_index = placing - (placing > dead_place).astype(jnp.int32)
    others = N_FSDP - 2
    share_rows = (INNER - CAP) // others
    extra_rows = INNER - CAP - share_rows * others
    rest_index = live_index - 1
    shifts = jax.random.randint(key_shift, (MATS, N_FSDP), 0, share_rows, dtype=jnp.int32)
    pair_shift = jnp.take_along_axis(shifts, jnp.clip(rest_index // 2, 0, N_FSDP - 1), axis=1)
    partnered = rest_index // 2 * 2 + 1 < others
    signed = jnp.where(rest_index % 2 == 0, -pair_shift, pair_shift)
    counts = share_rows + jnp.where(partnered, signed, 0) + (rest_index < extra_rows).astype(jnp.int32)
    counts = jnp.where(live_index == 0, CAP, counts)
    stale_count = jax.random.randint(key_stale, (MATS, N_FSDP), 1, CAP + 1, dtype=jnp.int32)
    stale_count = jnp.where(first_matrix, 1, stale_count).astype(jnp.int32)
    counts = jnp.where(is_dead, stale_count, counts).astype(jnp.int32)
    live_counts = counts * alive_flags[None, :]
    before = (placing[:, :, None] < placing[:, None, :]).astype(jnp.int32)
    offsets = jnp.sum(live_counts[:, :, None] * before, axis=1)
    stale_start = jax.random.randint(key_start, (MATS, N_FSDP), 0, INNER - stale_count + 1, dtype=jnp.int32)
    stale_start = jnp.where(first_matrix, INNER - 1, stale_start).astype(jnp.int32)
    offsets = jnp.where(is_dead, stale_start, offsets).astype(jnp.int32)
    return (alive_flags, counts, offsets)


def draw_momentum(key, part):
    return scaled_field(key, 11)


def draw_gradient(key, part):
    return scaled_field(key, 23)


def draw_live_ranks(key, part):
    return layout_tables(key)[0]


def draw_row_counts(key, part):
    return layout_tables(key)[1]


def draw_row_offsets(key, part):
    return layout_tables(key)[2]


def setup_inputs(seed: int = 0) -> dict:
    splits = jax.random.split(jax.random.key(seed), 7)
    momentum = draw_momentum(jax.random.fold_in(splits[6], 71), 0)
    gradient = draw_gradient(jax.random.fold_in(splits[6], 71), 0)
    live_ranks = draw_live_ranks(jax.random.fold_in(splits[6], 71), 0)
    owner_group = jax.random.permutation(splits[3], N_FSDP).astype(jnp.int32)
    row_counts = draw_row_counts(jax.random.fold_in(splits[6], 71), 0)
    row_offsets = draw_row_offsets(jax.random.fold_in(splits[6], 71), 0)
    return {"momentum": momentum, "gradient": gradient, "live_ranks": live_ranks, "owner_group": owner_group, "row_counts": row_counts, "row_offsets": row_offsets}


MOMENTUM_RATE = 0.95
QUINTIC_FIRST = 3.4445
QUINTIC_SECOND = -4.775
QUINTIC_THIRD = 2.0315
EPSILON = 1e-07
HIGHEST = lax.Precision.HIGHEST

def matmul(left_side, right_side):
    return jnp.dot(left_side, right_side, precision=HIGHEST, preferred_element_type=jnp.float32)

def orthogonalize(matrix):
    square_total = jnp.sum(matrix * matrix)
    iterate = matrix / (jnp.sqrt(square_total) + EPSILON)
    for repeat in range(ITERS):
        gram_now = lax.dot_general(iterate, iterate, (((1,), (1,)), ((), ())), precision=HIGHEST, preferred_element_type=jnp.float32)
        combined = QUINTIC_SECOND * gram_now + QUINTIC_THIRD * matmul(gram_now, gram_now)
        iterate = QUINTIC_FIRST * iterate + matmul(combined, iterate)
    return iterate * (0.2 * math.sqrt(max(INNER, WIDTH)))

def reference(momentum, gradient, live_ranks, owner_group, row_counts, row_offsets):
    position = jnp.arange(CAP, dtype=jnp.int32)

    def one_matrix(matrix_id):
        counts_now = row_counts[matrix_id] * live_ranks
        offsets_now = row_offsets[matrix_id]
        keep_grid = position[None, :] < counts_now[:, None]
        target = jnp.where(keep_grid, offsets_now[:, None] + position[None, :], INNER).reshape(-1).astype(jnp.int32)
        keep_slot = keep_grid.reshape(-1)[:, None]
        old_state = momentum[matrix_id]
        grad_now = gradient[matrix_id]
        fresh_slots = jnp.where(keep_slot, MOMENTUM_RATE * old_state + grad_now, 0.0)
        blended = grad_now + MOMENTUM_RATE * fresh_slots
        assembled = jnp.zeros((INNER, WIDTH), jnp.float32).at[target].add(blended, mode='drop')
        result = orthogonalize(assembled)
        picked = jnp.take(result, jnp.minimum(target, INNER - 1).astype(jnp.int32), axis=0)
        sent_back = jnp.where(keep_slot, picked, 0.0)
        return (fresh_slots, sent_back, result)
    fresh_all, back_all, results = lax.map(one_matrix, jnp.arange(MATS, dtype=jnp.int32))
    owned_rows = jnp.zeros_like(results).at[owner_group].set(results)
    return (fresh_all, back_all, owned_rows)
```

```python
import math

import jax
import jax.numpy as jnp
from jax import lax
from jax.sharding import PartitionSpec as P

WIDTH = 7168
INNER = 576

MOMENTUM_RATE = 0.95
QUINTIC_FIRST = 3.4445
QUINTIC_SECOND = -4.775
QUINTIC_THIRD = 2.0315
EPSILON = 1e-07
HIGH = lax.Precision.HIGH


def matmul(left_side, right_side, precision=HIGH):
    return jnp.dot(left_side, right_side, precision=precision, preferred_element_type=jnp.float32)


def on_device(momentum, gradient, live_ranks, owner_group, row_counts, row_offsets):
    rank_count = lax.axis_size("fsdp")
    my_rank = lax.axis_index("fsdp")
    slot_count = momentum.shape[1]
    columns = momentum.shape[2]
    matrices = owner_group.shape[0]
    rank_ids = jnp.arange(rank_count, dtype=jnp.int32)
    matrix_ids = jnp.arange(matrices, dtype=jnp.int32)
    owned_by = jnp.sum(
        matrix_ids[None, :] * (owner_group[None, :] == rank_ids[:, None]).astype(jnp.int32), axis=1
    )
    position = jnp.arange(slot_count, dtype=jnp.int32)
    counts = row_counts * live_ranks[None, :]
    my_counts = lax.dynamic_index_in_dim(counts, my_rank, 1, keepdims=False)
    valid = (position[None, :] < my_counts[:, None])[:, :, None]
    new_momentum = jnp.where(valid, MOMENTUM_RATE * momentum + gradient, 0.0)
    blended = jnp.where(valid, gradient + MOMENTUM_RATE * new_momentum, 0.0)
    blended_in = lax.all_to_all(
        jnp.take(blended, owned_by, axis=0), "fsdp", split_axis=0, concat_axis=0, tiled=True
    )
    owned_matrix = lax.dynamic_index_in_dim(owned_by, my_rank, 0, keepdims=False)
    source_counts = lax.dynamic_index_in_dim(counts, owned_matrix, 0, keepdims=False)
    source_offsets = lax.dynamic_index_in_dim(row_offsets, owned_matrix, 0, keepdims=False)
    keep_in = position[None, :] < source_counts[:, None]
    target = jnp.where(keep_in, source_offsets[:, None] + position[None, :], -1).reshape(-1)
    select = (target[None, :] == jnp.arange(INNER, dtype=jnp.int32)[:, None]).astype(jnp.float32)
    assembled = matmul(select, blended_in.reshape(-1, columns), lax.Precision.HIGHEST)
    gram = lax.dot_general(
        assembled,
        assembled,
        (((1,), (1,)), ((), ())),
        precision=HIGH,
        preferred_element_type=jnp.float32,
    )
    shares = lax.psum_scatter(gram, "tensor", scatter_dimension=0, tiled=True)
    gram = lax.all_gather(shares, "tensor", axis=0, tiled=True)
    inverse = 1.0 / (jnp.sqrt(jnp.trace(gram)) + EPSILON)
    gram = (gram * inverse) * inverse
    eye = jnp.eye(INNER, dtype=jnp.float32)

    def step(gram_now):
        return (
            QUINTIC_FIRST * eye
            + QUINTIC_SECOND * gram_now
            + QUINTIC_THIRD * matmul(gram_now, gram_now)
        )

    first = step(gram)
    second = step(matmul(matmul(first, gram), first))
    result = matmul(second, matmul(first, assembled * inverse)) * (
        0.2 * math.sqrt(max(INNER, WIDTH))
    )
    sent_back = lax.dot_general(
        select,
        result,
        (((0,), (0,)), ((), ())),
        precision=lax.Precision.HIGHEST,
        preferred_element_type=jnp.float32,
    ).reshape(rank_count, slot_count, columns)
    update_home = lax.all_to_all(sent_back, "fsdp", split_axis=0, concat_axis=0, tiled=True)
    update_shards = jnp.take(update_home, owner_group, axis=0)
    return (new_momentum, update_shards, result[None])


def solution(mesh):
    placed = (P(None, "fsdp", "tensor"), P(None, "fsdp", "tensor"), P(), P(), P(), P())
    return jax.shard_map(
        on_device,
        mesh=mesh,
        in_specs=placed,
        out_specs=(P(None, "fsdp", "tensor"), P(None, "fsdp", "tensor"), P("fsdp", None, "tensor")),
        check_vma=False,
    )
```

```python
import functools
import math

import jax
import jax.numpy as jnp
from jax import lax
from jax.experimental import pallas as pl
from jax.experimental.pallas import tpu as pltpu
from jax.sharding import PartitionSpec as P

WIDTH = 7168
INNER = 576
PADDED = 640
BLOCK = 64
LANES = 128

MOMENTUM_RATE = 0.95
QUINTIC_FIRST = 3.4445
QUINTIC_SECOND = -4.775
QUINTIC_THIRD = 2.0315
EPSILON = 1e-07
SCALE = 0.2 * math.sqrt(max(INNER, WIDTH))

MESH = pl.DeviceIdType.MESH
F32 = jnp.float32
BF16 = jnp.bfloat16

GRID = (8, 4, 2)


def dot(left, right):
    return jnp.dot(left, right, preferred_element_type=F32)


def iota(shape, axis):
    return lax.broadcasted_iota(jnp.int32, shape, axis)


def split(value):
    high = value.astype(BF16)
    low = (value - high.astype(F32)).astype(BF16)
    return high, low


def pack_slots(block):
    rows, columns = block.shape
    spare = LANES - columns
    wide = jnp.concatenate([block, jnp.zeros((rows, spare), F32)], axis=1)
    last = wide[rows - 8 :]
    pieces = []
    for tile in range((rows - 8) // 8):
        if tile * spare < columns:
            pieces.append(pltpu.roll(last, (columns - spare * tile) % LANES, 1))
        else:
            pieces.append(jnp.zeros((8, LANES), F32))
    tail = jnp.concatenate(pieces, axis=0)
    return jnp.where(iota(tail.shape, 1) < columns, wide[: rows - 8], tail)


def unpack_slots(packed, columns):
    spare = LANES - columns
    lane = iota((8, LANES), 1)
    last = jnp.zeros((8, LANES), F32)
    for tile in range(-(-columns // spare)):
        piece = pltpu.roll(packed[8 * tile : 8 * tile + 8], (spare * tile - columns) % LANES, 1)
        last = jnp.where((lane >= spare * tile) & (lane < spare * (tile + 1)), piece, last)
    main = jnp.where(iota(packed.shape, 1) < columns, packed, 0.0)
    return jnp.concatenate([main, last], axis=0)


def pack_gram(gram, store):
    lane = iota((BLOCK, LANES), 1)

    def tile(row, column):
        return gram[BLOCK * row : BLOCK * row + BLOCK, LANES * column : LANES * column + LANES]

    entry = 0
    for p in range(4):
        for column in range(p, 4):
            store(entry, tile(2 * p, column))
            entry += 1
        for column in range(p + 1, 4):
            store(entry, tile(2 * p + 1, column))
            entry += 1
        store(entry, jnp.where(lane < BLOCK, tile(2 * p, 4), tile(2 * p + 1, p)))
        entry += 1
    for row in (1, 5):
        store(entry, jnp.where(lane < BLOCK, tile(row, 4), pltpu.roll(tile(row + 2, 4), BLOCK, 1)))
        entry += 1
    store(entry, tile(8, 4))


ENTRIES = 23


def gram_entries():
    full, merged, entry = {}, {}, 0
    for p in range(4):
        for column in range(p, 4):
            full[2 * p, column] = entry
            entry += 1
        for column in range(p + 1, 4):
            full[2 * p + 1, column] = entry
            entry += 1
        merged[p] = entry
        entry += 1
    return full, merged, {1: entry, 5: entry + 1}, entry + 2


def gram_trace(load):
    full, merged, _, last = gram_entries()
    row, lane = iota((BLOCK, LANES), 0), iota((BLOCK, LANES), 1)
    diagonal = row == lane
    total = jnp.where(diagonal, load(last), 0.0)
    for p in range(4):
        total += jnp.where(diagonal, load(full[2 * p, p]), 0.0)
        total += jnp.where(row + BLOCK == lane, load(merged[p]), 0.0)
    return jnp.sum(total, axis=(0, 1), keepdims=True)


def unpack_gram(load, store):
    full, merged, edge, last = gram_entries()
    half = iota((BLOCK, LANES), 1) < BLOCK
    row, lane = iota((LANES, LANES), 0), iota((LANES, LANES), 1)
    for p in range(4):
        block = jnp.concatenate(
            [load(full[2 * p, p]), jnp.where(half, 0.0, load(merged[p]))], axis=0
        )
        store(p, p, jnp.where((row >= BLOCK) & (lane < BLOCK), block.T, block))
        for q in range(p + 1, 4):
            block = jnp.concatenate([load(full[2 * p, q]), load(full[2 * p + 1, q])], axis=0)
            store(p, q, block)
            store(q, p, block.T)
        odd = 2 * p + 1
        if odd in edge:
            right = load(edge[odd])
        else:
            right = pltpu.roll(load(edge[odd - 2]), BLOCK, 1)
        block = jnp.concatenate(
            [jnp.where(half, load(merged[p]), 0.0), jnp.where(half, right, 0.0)], axis=0
        )
        store(p, 4, block)
        store(4, p, block.T[:BLOCK])
    store(4, 4, jnp.where(half, load(last), 0.0))


def near_first(count):
    order = [0]
    for distance in range(1, count // 2 + 1):
        order.append(distance)
        if distance != count - distance:
            order.append(count - distance)
    return order


def step_kernel(
    ranks,
    grid,
    momentum,
    gradient,
    live,
    owners,
    counts,
    offsets,
    home,
    result,
    sent_in,
    came_in,
    sent_out,
    gathered,
    gram,
    part,
    other,
    row_sum,
    row_in,
    cell_sum,
    cell_in,
    whole,
    halves,
    column,
    kept,
    summed,
    in_send,
    in_recv,
    out_send,
    out_recv,
    core_send,
    core_recv,
    x_send,
    x_recv,
    y_send,
    y_recv,
):
    y_count, x_count, core_count = grid
    matrices, slots, columns = momentum.shape
    me = lax.axis_index("fsdp")
    here = lax.axis_index("tensor")
    core = lax.rem(here, core_count)
    x_here = lax.rem(here // core_count, x_count)
    y_here = here // (core_count * x_count)

    def rank_at(distance):
        return {"fsdp": lax.rem(me + distance, ranks), "tensor": here}

    def cell(y, x, c):
        return {"fsdp": me, "tensor": (y * x_count + x) * core_count + c}

    sibling = cell(y_here, x_here, 1 - core)
    x_peers = [cell(y_here, lax.rem(x_here + d, x_count), core) for d in range(1, x_count)]
    y_peers = [cell(lax.rem(y_here + d, y_count), x_here, core) for d in range(1, y_count)]

    barrier = pltpu.get_barrier_semaphore()
    peers = [rank_at(d) for d in range(1, ranks)] + [sibling] + x_peers + y_peers
    for peer in peers:
        pl.semaphore_signal(barrier, inc=1, device_id=peer, device_id_type=MESH)

    def owned_by(rank):
        found = jnp.int32(0)
        for k in range(matrices):
            found = jnp.where(owners[k] == rank, k, found)
        return found

    mine = owned_by(me)
    for d in range(ranks):
        k = mine if d == 0 else owned_by(lax.rem(me + d, ranks))
        grad = gradient[k]
        blended = grad + MOMENTUM_RATE * (MOMENTUM_RATE * momentum[k] + grad)
        if d == 0:
            came_in[0] = pack_slots(blended)
        else:
            sent_in[d] = pack_slots(blended)

    pl.semaphore_wait(barrier, len(peers))

    order = near_first(ranks)
    copies_in = {}
    for d in order[:0:-1]:
        copies_in[d] = pltpu.make_async_remote_copy(
            src_ref=sent_in.at[d],
            dst_ref=came_in.at[d],
            send_sem=in_send.at[d],
            recv_sem=in_recv.at[d],
            device_id=rank_at(d),
            device_id_type=MESH,
        )
        copies_in[d].start()

    def held(rank):
        return offsets[mine, rank], counts[mine, rank] * live[rank]

    for pair in range(ranks // 2):
        blocks, tables = [], []
        for d in order[2 * pair : 2 * pair + 2]:
            if d > 0:
                copies_in[d].wait_recv()
            blocks.append(unpack_slots(came_in[d], columns))
            tables.append(held(lax.rem(me + ranks - d, ranks)))
        data = jnp.concatenate(split(jnp.concatenate(blocks, axis=0)), axis=1)
        lane = iota((INNER, 2 * slots), 1)
        first = lane < slots
        slot = jnp.where(first, lane, lane - slots)
        offset = jnp.where(first, tables[0][0], tables[1][0])
        count = jnp.where(first, tables[0][1], tables[1][1])
        select = (iota((INNER, 2 * slots), 0) - slot == offset) & (slot < count)
        added = dot(jnp.where(select, 1.0, 0.0).astype(BF16), data)
        if pair == 0:
            gathered[...] = added
        else:
            gathered[...] += added

    both = gathered[...].astype(BF16)
    high, low = both[:, :LANES], both[:, LANES:]
    pad = jnp.zeros((PADDED - INNER, 4 * LANES), BF16)
    left = jnp.concatenate([both, both], axis=1)
    right = jnp.concatenate([jnp.concatenate([high, high, low, low], axis=1), pad], axis=0)
    across = (((1,), (1,)), ((), ()))
    cut = 2 * LANES
    gram[:cut, :] = lax.dot_general(left[:cut], right, across, preferred_element_type=F32)
    gram[cut:, cut:] = lax.dot_general(left[cut:], right[cut:], across, preferred_element_type=F32)

    def put(entry, tile):
        part[BLOCK * entry : BLOCK * entry + BLOCK, :] = tile

    pack_gram(gram, put)
    total_rows = part.shape[0]
    if total_rows > BLOCK * ENTRIES:
        part[BLOCK * ENTRIES :, :] = jnp.zeros((total_rows - BLOCK * ENTRIES, LANES), F32)

    piece = total_rows // (core_count * y_count * x_count)

    def place(ref, index, count=1):
        size = piece * count
        return ref.at[pl.ds(pl.multiple_of(index * piece, 8), size), :]

    pending = []

    def send(src, dst, peer, send_sem, recv_sem):
        copy = pltpu.make_async_remote_copy(
            src_ref=src,
            dst_ref=dst,
            send_sem=send_sem,
            recv_sem=recv_sem,
            device_id=peer,
            device_id_type=MESH,
        )
        copy.start()
        pending.append(copy)
        return copy

    cells = y_count * x_count
    y_order = near_first(y_count)
    x_order = near_first(x_count)[1:]

    def y_at(d):
        return lax.rem(y_here + d, y_count)

    def x_at(d):
        return lax.rem(x_here + d, x_count)

    copies = {}
    for d in y_order[::-1]:
        line = y_at(d) * x_count
        copies[d] = send(
            place(part, (1 - core) * cells + line, x_count),
            place(other, line, x_count),
            sibling,
            core_send.at[d],
            core_recv.at[d],
        )
    x_copies = {}
    for d in y_order[::-1]:
        line = y_at(d) * x_count
        copies[d].wait_recv()
        place(row_sum, line, x_count)[...] = (
            place(part, core * cells + line, x_count)[...] + place(other, line, x_count)[...]
        )
        for e in x_order[::-1]:
            slot = d * x_count + e
            x_copies[d, e] = send(
                place(row_sum, line + x_at(e)),
                row_in.at[slot],
                x_peers[e - 1],
                x_send.at[slot],
                x_recv.at[slot],
            )
    y_copies = {}
    for d in y_order[::-1]:
        total = place(row_sum, y_at(d) * x_count + x_here)[...]
        for e in x_order:
            x_copies[d, e].wait_recv()
            total = total + row_in[d * x_count + e]
        if d == 0:
            own_total = total
        else:
            cell_sum[d] = total
            y_copies[d] = send(
                cell_sum.at[d], cell_in.at[d], y_peers[d - 1], y_send.at[d], y_recv.at[d]
            )
    total = own_total
    for d in y_order[1:]:
        y_copies[d].wait_recv()
        total = total + cell_in[d]

    def home_of(d, e):
        return place(whole, core * cells + y_at(d) * x_count + x_at(e))

    home_of(0, 0)[...] = total
    for d in y_order[:0:-1]:
        y_copies[d] = send(
            home_of(0, 0),
            home_of(0, 0),
            y_peers[d - 1],
            y_send.at[y_count + d],
            y_recv.at[y_count + d],
        )
    core_copies = []
    for d in y_order:
        back = lax.rem(y_count - d, y_count)
        if d > 0:
            y_copies[d].wait_recv()
        for e in x_order[::-1]:
            slot = (y_count + d) * x_count + e
            x_copies[d, e] = send(
                home_of(back, 0),
                home_of(back, 0),
                x_peers[e - 1],
                x_send.at[slot],
                x_recv.at[slot],
            )
        slot = y_count + d * x_count
        core_copies.append(
            send(
                home_of(back, 0), home_of(back, 0), sibling, core_send.at[slot], core_recv.at[slot]
            )
        )
    for d in y_order:
        back = lax.rem(y_count - d, y_count)
        for e in x_order:
            x_copies[d, e].wait_recv()
            source = home_of(back, x_count - e)
            slot = y_count + d * x_count + e
            core_copies.append(
                send(source, source, sibling, core_send.at[slot], core_recv.at[slot])
            )
    for copy in core_copies:
        copy.wait_recv()

    def load(entry):
        return whole[BLOCK * entry : BLOCK * entry + BLOCK, :]

    inverse = 1.0 / (jnp.sqrt(gram_trace(load)) + EPSILON)

    def keep(p, q, block):
        high, low = split((block * inverse) * inverse)
        rows, lanes = slice(LANES * p, LANES * p + block.shape[0]), LANES * q
        halves[rows, lanes : lanes + LANES] = high
        halves[rows, PADDED + lanes : PADDED + lanes + LANES] = low

    unpack_gram(load, keep)

    for base in (0, PADDED):
        column[base + INNER : base + PADDED, :] = jnp.zeros((PADDED - INNER, 2 * LANES), BF16)

    def stack(value):
        both = jnp.concatenate(split(value), axis=1)
        column[:INNER, :] = both
        column[PADDED : PADDED + INNER, :] = both

    start = (gathered[:, :LANES] + gathered[:, LANES:]) * inverse
    kept[...] = start
    summed[...] = jnp.zeros_like(start)
    stack(start)

    @pl.loop(0, 12)
    def _(index):
        phase = lax.rem(index + 3, 5)
        opens = (phase == 3) | (phase == 1)
        closes = (phase == 4) | (phase == 2)
        keep_part = jnp.where(opens, QUINTIC_SECOND, jnp.where(closes, QUINTIC_FIRST, 0.0))
        product_part = jnp.where(opens, QUINTIC_THIRD, 1.0)
        sum_part = jnp.where(
            index == 1,
            QUINTIC_FIRST,
            jnp.where(index == 6, QUINTIC_SECOND, jnp.where(index == 11, QUINTIC_THIRD, 0.0)),
        )
        product = dot(halves[...], column[...])
        value = keep_part * kept[...] + product_part * (product[:, :LANES] + product[:, LANES:])
        stack(value)
        kept[...] = jnp.where(opens, kept[...], value)
        summed[...] += sum_part * value

    final = summed[...] * SCALE
    result[...] = final
    stack(final)
    sent = column[:PADDED, :]
    backward = order[::-1]
    copies_out = []
    for pair in range(ranks // 2):
        ds = backward[2 * pair : 2 * pair + 2]
        tables = [held(lax.rem(me + d, ranks)) for d in ds]
        row = iota((2 * slots, PADDED), 0)
        first = row < slots
        slot = jnp.where(first, row, row - slots)
        offset = jnp.where(first, tables[0][0], tables[1][0])
        count = jnp.where(first, tables[0][1], tables[1][1])
        select = (iota((2 * slots, PADDED), 1) - slot == offset) & (slot < count)
        picked = dot(jnp.where(select, 1.0, 0.0).astype(BF16), sent)
        picked = (picked[:, :LANES] + picked[:, LANES:])[:, :columns]
        for place, d in enumerate(ds):
            packed = pack_slots(picked[place * slots : place * slots + slots])
            if d == 0:
                home[0] = packed
                continue
            sent_out[d] = packed
            copy = pltpu.make_async_remote_copy(
                src_ref=sent_out.at[d],
                dst_ref=home.at[d],
                send_sem=out_send.at[d],
                recv_sem=out_recv.at[d],
                device_id=rank_at(d),
                device_id_type=MESH,
            )
            copy.start()
            copies_out.append(copy)
    for copy in copies_out:
        copy.wait_recv()
    for copy in list(copies_in.values()) + pending + copies_out:
        copy.wait_send()


def finish_kernel(ranks, columns, home, result, owners, update, owned):
    me = lax.axis_index("fsdp")
    for k in range(update.shape[0]):
        source = lax.rem(me + ranks - owners[k], ranks)
        update[k] = unpack_slots(home[source], columns)[:, :columns]
    owned[0] = result[:, :columns]


def on_device(ranks, grid, momentum, gradient, live_ranks, owner_group, row_counts, row_offsets):
    y_count, x_count, core_count = grid
    matrices, slots, columns = momentum.shape
    cells = y_count * x_count * core_count
    piece = -(-8 * ENTRIES // cells) * 8
    total_rows = piece * cells
    half_rows = total_rows // core_count

    vmem = pl.BlockSpec(memory_space=pltpu.VMEM)
    smem = pl.BlockSpec(memory_space=pltpu.SMEM)
    packed = (ranks, slots - 8, LANES)
    dma = pltpu.SemaphoreType.DMA
    home, result = pl.pallas_call(
        functools.partial(step_kernel, ranks, grid),
        out_shape=(jax.ShapeDtypeStruct(packed, F32), jax.ShapeDtypeStruct((INNER, LANES), F32)),
        in_specs=[vmem, vmem, smem, smem, smem, smem],
        out_specs=(vmem, vmem),
        scratch_shapes=[
            pltpu.VMEM(packed, F32),
            pltpu.VMEM(packed, F32),
            pltpu.VMEM(packed, F32),
            pltpu.VMEM((INNER, 2 * LANES), F32),
            pltpu.VMEM((INNER, PADDED), F32),
            pltpu.VMEM((total_rows, LANES), F32),
            pltpu.VMEM((half_rows, LANES), F32),
            pltpu.VMEM((half_rows, LANES), F32),
            pltpu.VMEM((y_count * x_count, piece, LANES), F32),
            pltpu.VMEM((y_count, piece, LANES), F32),
            pltpu.VMEM((y_count, piece, LANES), F32),
            pltpu.VMEM((total_rows, LANES), F32),
            pltpu.VMEM((INNER, 2 * PADDED), BF16),
            pltpu.VMEM((2 * PADDED, 2 * LANES), BF16),
            pltpu.VMEM((INNER, LANES), F32),
            pltpu.VMEM((INNER, LANES), F32),
            dma((ranks,)),
            dma((ranks,)),
            dma((ranks,)),
            dma((ranks,)),
            dma((y_count * (1 + x_count),)),
            dma((y_count * (1 + x_count),)),
            dma((2 * y_count * x_count,)),
            dma((2 * y_count * x_count,)),
            dma((2 * y_count,)),
            dma((2 * y_count,)),
        ],
        compiler_params=pltpu.CompilerParams(collective_id=0, has_side_effects=True),
        name="muon_exchange",
    )(momentum, gradient, live_ranks, owner_group, row_counts, row_offsets)

    update_shards, owned_update = pl.pallas_call(
        functools.partial(finish_kernel, ranks, columns),
        out_shape=(
            jax.ShapeDtypeStruct(momentum.shape, F32),
            jax.ShapeDtypeStruct((1, INNER, columns), F32),
        ),
        in_specs=[vmem, vmem, smem],
        out_specs=(vmem, vmem),
        name="muon_finish",
    )(home, result, owner_group)

    my_rank = lax.axis_index("fsdp")
    my_counts = lax.dynamic_index_in_dim(row_counts * live_ranks[None, :], my_rank, 1, keepdims=False)
    valid = jnp.arange(slots, dtype=jnp.int32)[None, :] < my_counts[:, None]
    new_momentum = jnp.where(valid[:, :, None], MOMENTUM_RATE * momentum + gradient, 0.0)
    return (new_momentum, update_shards, owned_update)


def solution(mesh, grid=GRID):
    placed = (P(None, "fsdp", "tensor"), P(None, "fsdp", "tensor"), P(), P(), P(), P())
    return jax.shard_map(
        functools.partial(on_device, mesh.shape["fsdp"], grid),
        mesh=mesh,
        in_specs=placed,
        out_specs=(P(None, "fsdp", "tensor"), P(None, "fsdp", "tensor"), P("fsdp", None, "tensor")),
        check_vma=False,
    )
```

```python
import functools
import math

import jax
import jax.numpy as jnp
from jax import lax
from jax.experimental import pallas as pl
from jax.experimental.pallas import tpu as pltpu
from jax.sharding import PartitionSpec as P

WIDTH = 7168
INNER = 576
PADDED = 640
BLOCK = 64
LANES = 128

MOMENTUM_RATE = 0.95
QUINTIC_FIRST = 3.4445
QUINTIC_SECOND = -4.775
QUINTIC_THIRD = 2.0315
EPSILON = 1e-07
SCALE = 0.2 * math.sqrt(max(INNER, WIDTH))

VMEM_LIMIT = 32 * 1024 * 1024

MESH = pl.DeviceIdType.MESH
F32 = jnp.float32
BF16 = jnp.bfloat16

GRID = (8, 4, 2)


def dot(left, right):
    return jnp.dot(left, right, preferred_element_type=F32)


def iota(shape, axis):
    return lax.broadcasted_iota(jnp.int32, shape, axis)


def split(value):
    high = value.astype(BF16)
    low = (value - high.astype(F32)).astype(BF16)
    return high, low


def pack_slots(block):
    rows, columns = block.shape
    spare = LANES - columns
    wide = jnp.concatenate([block, jnp.zeros((rows, spare), F32)], axis=1)
    last = wide[rows - 8 :]
    pieces = []
    for tile in range((rows - 8) // 8):
        if tile * spare < columns:
            pieces.append(pltpu.roll(last, (columns - spare * tile) % LANES, 1))
        else:
            pieces.append(jnp.zeros((8, LANES), F32))
    tail = jnp.concatenate(pieces, axis=0)
    return jnp.where(iota(tail.shape, 1) < columns, wide[: rows - 8], tail)


def unpack_slots(packed, columns):
    spare = LANES - columns
    lane = iota((8, LANES), 1)
    last = jnp.zeros((8, LANES), F32)
    for tile in range(-(-columns // spare)):
        piece = pltpu.roll(packed[8 * tile : 8 * tile + 8], (spare * tile - columns) % LANES, 1)
        last = jnp.where((lane >= spare * tile) & (lane < spare * (tile + 1)), piece, last)
    main = jnp.where(iota(packed.shape, 1) < columns, packed, 0.0)
    return jnp.concatenate([main, last], axis=0)


def pack_gram(gram, store):
    lane = iota((BLOCK, LANES), 1)

    def tile(row, column):
        return gram[BLOCK * row : BLOCK * row + BLOCK, LANES * column : LANES * column + LANES]

    entry = 0
    for p in range(4):
        for column in range(p, 4):
            store(entry, tile(2 * p, column))
            entry += 1
        for column in range(p + 1, 4):
            store(entry, tile(2 * p + 1, column))
            entry += 1
        store(entry, jnp.where(lane < BLOCK, tile(2 * p, 4), tile(2 * p + 1, p)))
        entry += 1
    for row in (1, 5):
        store(entry, jnp.where(lane < BLOCK, tile(row, 4), pltpu.roll(tile(row + 2, 4), BLOCK, 1)))
        entry += 1
    store(entry, tile(8, 4))


ENTRIES = 23


def gram_entries():
    full, merged, entry = {}, {}, 0
    for p in range(4):
        for column in range(p, 4):
            full[2 * p, column] = entry
            entry += 1
        for column in range(p + 1, 4):
            full[2 * p + 1, column] = entry
            entry += 1
        merged[p] = entry
        entry += 1
    return full, merged, {1: entry, 5: entry + 1}, entry + 2


def gram_trace(load):
    full, merged, _, last = gram_entries()
    row, lane = iota((BLOCK, LANES), 0), iota((BLOCK, LANES), 1)
    diagonal = row == lane
    total = jnp.where(diagonal, load(last), 0.0)
    for p in range(4):
        total += jnp.where(diagonal, load(full[2 * p, p]), 0.0)
        total += jnp.where(row + BLOCK == lane, load(merged[p]), 0.0)
    return jnp.sum(total, axis=(0, 1), keepdims=True)


def unpack_gram(load, store):
    full, merged, edge, last = gram_entries()
    half = iota((BLOCK, LANES), 1) < BLOCK
    row, lane = iota((LANES, LANES), 0), iota((LANES, LANES), 1)
    for p in range(4):
        block = jnp.concatenate(
            [load(full[2 * p, p]), jnp.where(half, 0.0, load(merged[p]))], axis=0
        )
        store(p, p, jnp.where((row >= BLOCK) & (lane < BLOCK), block.T, block))
        for q in range(p + 1, 4):
            block = jnp.concatenate([load(full[2 * p, q]), load(full[2 * p + 1, q])], axis=0)
            store(p, q, block)
            store(q, p, block.T)
        odd = 2 * p + 1
        if odd in edge:
            right = load(edge[odd])
        else:
            right = pltpu.roll(load(edge[odd - 2]), BLOCK, 1)
        block = jnp.concatenate(
            [jnp.where(half, load(merged[p]), 0.0), jnp.where(half, right, 0.0)], axis=0
        )
        store(p, 4, block)
        store(4, p, block.T[:BLOCK])
    store(4, 4, jnp.where(half, load(last), 0.0))


def near_first(count):
    order = [0]
    for distance in range(1, count // 2 + 1):
        order.append(distance)
        if distance != count - distance:
            order.append(count - distance)
    return order


def step_kernel(
    ranks,
    grid,
    momentum_out,
    gradient_out,
    live_out,
    owners_out,
    counts_out,
    offsets_out,
    home,
    result,
    fresh,
    sent_in,
    came_in,
    sent_out,
    gathered,
    gram,
    part,
    other,
    row_sum,
    row_in,
    cell_sum,
    cell_in,
    whole,
    halves,
    column,
    kept,
    summed,
    in_send,
    in_recv,
    out_send,
    out_recv,
    core_send,
    core_recv,
    x_send,
    x_recv,
    y_send,
    y_recv,
    momentum,
    gradient,
    live,
    owners,
    counts,
    offsets,
    loads,
):
    y_count, x_count, core_count = grid
    matrices, slots, columns = momentum.shape
    me = lax.axis_index("fsdp")
    here = lax.axis_index("tensor")
    core = lax.rem(here, core_count)
    x_here = lax.rem(here // core_count, x_count)
    y_here = here // (core_count * x_count)

    def rank_at(distance):
        return {"fsdp": lax.rem(me + distance, ranks), "tensor": here}

    def cell(y, x, c):
        return {"fsdp": me, "tensor": (y * x_count + x) * core_count + c}

    sibling = cell(y_here, x_here, 1 - core)
    x_peers = [cell(y_here, lax.rem(x_here + d, x_count), core) for d in range(1, x_count)]
    y_peers = [cell(lax.rem(y_here + d, y_count), x_here, core) for d in range(1, y_count)]

    barrier = pltpu.get_barrier_semaphore()
    peers = [rank_at(d) for d in range(1, ranks)] + [sibling] + x_peers + y_peers
    for peer in peers:
        pl.semaphore_signal(barrier, inc=1, device_id=peer, device_id_type=MESH)

    inputs = (
        (live_out, live),
        (owners_out, owners),
        (counts_out, counts),
        (offsets_out, offsets),
        (momentum_out, momentum),
        (gradient_out, gradient),
    )
    loading = [
        pltpu.make_async_copy(source, target, loads.at[n])
        for n, (source, target) in enumerate(inputs)
    ]
    for load in loading:
        load.start()
    for load in loading:
        load.wait()

    def owned_by(rank):
        found = jnp.int32(0)
        for k in range(matrices):
            found = jnp.where(owners[k] == rank, k, found)
        return found

    mine = owned_by(me)
    for d in range(ranks):
        k = mine if d == 0 else owned_by(lax.rem(me + d, ranks))
        grad = gradient[k]
        blended = grad + MOMENTUM_RATE * (MOMENTUM_RATE * momentum[k] + grad)
        if d == 0:
            came_in[0] = pack_slots(blended)
        else:
            sent_in[d] = pack_slots(blended)

    pl.semaphore_wait(barrier, len(peers))

    def copy_in(d):
        return pltpu.make_async_remote_copy(
            src_ref=sent_in.at[d],
            dst_ref=came_in.at[d],
            send_sem=in_send.at[d],
            recv_sem=in_recv.at[d],
            device_id=rank_at(d),
            device_id_type=MESH,
        )

    order = near_first(ranks)
    copies_in = {d: copy_in(d) for d in range(1, ranks)}
    for d in order[:0:-1]:
        copies_in[d].start()

    rows = iota((slots, columns), 0)
    for k in range(matrices):
        updated = MOMENTUM_RATE * momentum[k] + gradient[k]
        fresh[k] = jnp.where(rows < counts[k, me] * live[me], updated, 0.0)

    def held(rank):
        return offsets[mine, rank], counts[mine, rank] * live[rank]

    for pair in range(ranks // 2):
        blocks, tables = [], []
        for rank in (2 * pair, 2 * pair + 1):
            d = lax.rem(me + ranks - rank, ranks)

            @pl.when(d > 0)
            def _():
                copy_in(d).wait_recv()

            blocks.append(unpack_slots(came_in[d], columns))
            tables.append(held(rank))
        data = jnp.concatenate(split(jnp.concatenate(blocks, axis=0)), axis=1)
        lane = iota((INNER, 2 * slots), 1)
        first = lane < slots
        slot = jnp.where(first, lane, lane - slots)
        offset = jnp.where(first, tables[0][0], tables[1][0])
        count = jnp.where(first, tables[0][1], tables[1][1])
        select = (iota((INNER, 2 * slots), 0) - slot == offset) & (slot < count)
        added = dot(jnp.where(select, 1.0, 0.0).astype(BF16), data)
        if pair == 0:
            gathered[...] = added
        else:
            gathered[...] += added

    both = gathered[...].astype(BF16)
    high, low = both[:, :LANES], both[:, LANES:]
    pad = jnp.zeros((PADDED - INNER, 4 * LANES), BF16)
    left = jnp.concatenate([both, both], axis=1)
    right = jnp.concatenate([jnp.concatenate([high, high, low, low], axis=1), pad], axis=0)
    across = (((1,), (1,)), ((), ()))
    cut = 2 * LANES
    gram[:cut, :] = lax.dot_general(left[:cut], right, across, preferred_element_type=F32)
    gram[cut:, cut:] = lax.dot_general(left[cut:], right[cut:], across, preferred_element_type=F32)

    def put(entry, tile):
        part[BLOCK * entry : BLOCK * entry + BLOCK, :] = tile

    pack_gram(gram, put)
    total_rows = part.shape[0]
    if total_rows > BLOCK * ENTRIES:
        part[BLOCK * ENTRIES :, :] = jnp.zeros((total_rows - BLOCK * ENTRIES, LANES), F32)

    piece = total_rows // (core_count * y_count * x_count)

    def place(ref, index, count=1):
        size = piece * count
        return ref.at[pl.ds(pl.multiple_of(index * piece, 8), size), :]

    pending = []

    def send(src, dst, peer, send_sem, recv_sem):
        copy = pltpu.make_async_remote_copy(
            src_ref=src,
            dst_ref=dst,
            send_sem=send_sem,
            recv_sem=recv_sem,
            device_id=peer,
            device_id_type=MESH,
        )
        copy.start()
        pending.append(copy)
        return copy

    cells = y_count * x_count
    y_order = near_first(y_count)
    x_order = near_first(x_count)[1:]

    def y_at(d):
        return lax.rem(y_here + d, y_count)

    def x_at(d):
        return lax.rem(x_here + d, x_count)

    copies = {}
    for d in y_order[::-1]:
        line = y_at(d) * x_count
        copies[d] = send(
            place(part, (1 - core) * cells + line, x_count),
            place(other, line, x_count),
            sibling,
            core_send.at[d],
            core_recv.at[d],
        )
    x_copies = {}
    for d in y_order[::-1]:
        line = y_at(d) * x_count
        copies[d].wait_recv()
        place(row_sum, line, x_count)[...] = (
            place(part, core * cells + line, x_count)[...] + place(other, line, x_count)[...]
        )
        for e in x_order[::-1]:
            slot = d * x_count + e
            x_copies[d, e] = send(
                place(row_sum, line + x_at(e)),
                row_in.at[slot],
                x_peers[e - 1],
                x_send.at[slot],
                x_recv.at[slot],
            )
    y_copies = {}
    for d in y_order[::-1]:
        total = place(row_sum, y_at(d) * x_count + x_here)[...]
        for e in x_order:
            x_copies[d, e].wait_recv()
            total = total + row_in[d * x_count + e]
        if d == 0:
            own_total = total
        else:
            cell_sum[d] = total
            y_copies[d] = send(
                cell_sum.at[d], cell_in.at[d], y_peers[d - 1], y_send.at[d], y_recv.at[d]
            )
    total = own_total
    for d in y_order[1:]:
        y_copies[d].wait_recv()
        total = total + cell_in[d]

    def home_of(d, e):
        return place(whole, core * cells + y_at(d) * x_count + x_at(e))

    home_of(0, 0)[...] = total
    for d in y_order[:0:-1]:
        y_copies[d] = send(
            home_of(0, 0),
            home_of(0, 0),
            y_peers[d - 1],
            y_send.at[y_count + d],
            y_recv.at[y_count + d],
        )
    core_copies = []
    for d in y_order:
        back = lax.rem(y_count - d, y_count)
        if d > 0:
            y_copies[d].wait_recv()
        for e in x_order[::-1]:
            slot = (y_count + d) * x_count + e
            x_copies[d, e] = send(
                home_of(back, 0),
                home_of(back, 0),
                x_peers[e - 1],
                x_send.at[slot],
                x_recv.at[slot],
            )
        slot = y_count + d * x_count
        core_copies.append(
            send(
                home_of(back, 0), home_of(back, 0), sibling, core_send.at[slot], core_recv.at[slot]
            )
        )
    for d in y_order:
        back = lax.rem(y_count - d, y_count)
        for e in x_order:
            x_copies[d, e].wait_recv()
            source = home_of(back, x_count - e)
            slot = y_count + d * x_count + e
            core_copies.append(
                send(source, source, sibling, core_send.at[slot], core_recv.at[slot])
            )
    for copy in core_copies:
        copy.wait_recv()

    def load(entry):
        return whole[BLOCK * entry : BLOCK * entry + BLOCK, :]

    inverse = 1.0 / (jnp.sqrt(gram_trace(load)) + EPSILON)

    def keep(p, q, block):
        high, low = split((block * inverse) * inverse)
        rows, lanes = slice(LANES * p, LANES * p + block.shape[0]), LANES * q
        halves[rows, lanes : lanes + LANES] = high
        halves[rows, PADDED + lanes : PADDED + lanes + LANES] = low

    unpack_gram(load, keep)

    for base in (0, PADDED):
        column[base + INNER : base + PADDED, :] = jnp.zeros((PADDED - INNER, 2 * LANES), BF16)

    def stack(value):
        both = jnp.concatenate(split(value), axis=1)
        column[:INNER, :] = both
        column[PADDED : PADDED + INNER, :] = both

    start = (gathered[:, :LANES] + gathered[:, LANES:]) * inverse
    kept[...] = start
    summed[...] = jnp.zeros_like(start)
    stack(start)

    @pl.loop(0, 12)
    def _(index):
        phase = lax.rem(index + 3, 5)
        opens = (phase == 3) | (phase == 1)
        closes = (phase == 4) | (phase == 2)
        keep_part = jnp.where(opens, QUINTIC_SECOND, jnp.where(closes, QUINTIC_FIRST, 0.0))
        product_part = jnp.where(opens, QUINTIC_THIRD, 1.0)
        sum_part = jnp.where(
            index == 1,
            QUINTIC_FIRST,
            jnp.where(index == 6, QUINTIC_SECOND, jnp.where(index == 11, QUINTIC_THIRD, 0.0)),
        )
        product = dot(halves[...], column[...])
        value = keep_part * kept[...] + product_part * (product[:, :LANES] + product[:, LANES:])
        stack(value)
        kept[...] = jnp.where(opens, kept[...], value)
        summed[...] += sum_part * value

    final = summed[...] * SCALE
    result[...] = final
    stack(final)
    sent = column[:PADDED, :]
    backward = order[::-1]
    copies_out = []
    for pair in range(ranks // 2):
        ds = backward[2 * pair : 2 * pair + 2]
        tables = [held(lax.rem(me + d, ranks)) for d in ds]
        row = iota((2 * slots, PADDED), 0)
        first = row < slots
        slot = jnp.where(first, row, row - slots)
        offset = jnp.where(first, tables[0][0], tables[1][0])
        count = jnp.where(first, tables[0][1], tables[1][1])
        select = (iota((2 * slots, PADDED), 1) - slot == offset) & (slot < count)
        picked = dot(jnp.where(select, 1.0, 0.0).astype(BF16), sent)
        picked = (picked[:, :LANES] + picked[:, LANES:])[:, :columns]
        for place, d in enumerate(ds):
            packed = pack_slots(picked[place * slots : place * slots + slots])
            if d == 0:
                home[0] = packed
                continue
            sent_out[d] = packed
            copy = pltpu.make_async_remote_copy(
                src_ref=sent_out.at[d],
                dst_ref=home.at[d],
                send_sem=out_send.at[d],
                recv_sem=out_recv.at[d],
                device_id=rank_at(d),
                device_id_type=MESH,
            )
            copy.start()
            copies_out.append(copy)
    for copy in copies_out:
        copy.wait_recv()
    for copy in list(copies_in.values()) + pending + copies_out:
        copy.wait_send()


def finish_kernel(
    ranks,
    columns,
    home,
    result,
    fresh,
    owners_out,
    new_momentum,
    update,
    owned,
    update_here,
    owned_here,
    owners,
    sems,
):
    me = lax.axis_index("fsdp")
    load = pltpu.make_async_copy(owners_out, owners, sems.at[4])
    load.start()
    copies = [pltpu.make_async_copy(fresh, new_momentum, sems.at[0])]
    copies[0].start()
    owned_here[0] = result[...].T[:columns]
    copies.append(pltpu.make_async_copy(owned_here, owned, sems.at[1]))
    copies[1].start()
    load.wait()
    half = update.shape[0] // 2
    for k in range(update.shape[0]):
        source = lax.rem(me + ranks - owners[k], ranks)
        update_here[k] = unpack_slots(home[source], columns)[:, :columns]
        if k + 1 in (half, 2 * half):
            part = pl.ds(k + 1 - half, half)
            copies.append(
                pltpu.make_async_copy(
                    update_here.at[part], update.at[part], sems.at[2 + k // half]
                )
            )
            copies[-1].start()
    for copy in copies:
        copy.wait()


def on_device(ranks, grid, momentum, gradient, live_ranks, owner_group, row_counts, row_offsets):
    y_count, x_count, core_count = grid
    matrices, slots, columns = momentum.shape
    cells = y_count * x_count * core_count
    piece = -(-8 * ENTRIES // cells) * 8
    total_rows = piece * cells
    half_rows = total_rows // core_count

    vmem = pl.BlockSpec(memory_space=pltpu.VMEM)
    hbm = pl.BlockSpec(memory_space=pltpu.HBM)
    packed = (ranks, slots - 8, LANES)
    dma = pltpu.SemaphoreType.DMA
    operands = (momentum, gradient, live_ranks, owner_group, row_counts, row_offsets)
    home, result, fresh = pl.pallas_call(
        functools.partial(step_kernel, ranks, grid),
        out_shape=(
            jax.ShapeDtypeStruct(packed, F32),
            jax.ShapeDtypeStruct((INNER, LANES), F32),
            jax.ShapeDtypeStruct(momentum.shape, F32),
        ),
        in_specs=[hbm] * 6,
        out_specs=(vmem, vmem, vmem),
        scratch_shapes=[
            pltpu.VMEM(packed, F32),
            pltpu.VMEM(packed, F32),
            pltpu.VMEM(packed, F32),
            pltpu.VMEM((INNER, 2 * LANES), F32),
            pltpu.VMEM((INNER, PADDED), F32),
            pltpu.VMEM((total_rows, LANES), F32),
            pltpu.VMEM((half_rows, LANES), F32),
            pltpu.VMEM((half_rows, LANES), F32),
            pltpu.VMEM((y_count * x_count, piece, LANES), F32),
            pltpu.VMEM((y_count, piece, LANES), F32),
            pltpu.VMEM((y_count, piece, LANES), F32),
            pltpu.VMEM((total_rows, LANES), F32),
            pltpu.VMEM((INNER, 2 * PADDED), BF16),
            pltpu.VMEM((2 * PADDED, 2 * LANES), BF16),
            pltpu.VMEM((INNER, LANES), F32),
            pltpu.VMEM((INNER, LANES), F32),
            dma((ranks,)),
            dma((ranks,)),
            dma((ranks,)),
            dma((ranks,)),
            dma((y_count * (1 + x_count),)),
            dma((y_count * (1 + x_count),)),
            dma((2 * y_count * x_count,)),
            dma((2 * y_count * x_count,)),
            dma((2 * y_count,)),
            dma((2 * y_count,)),
            pltpu.VMEM(momentum.shape, F32),
            pltpu.VMEM(gradient.shape, F32),
            pltpu.SMEM(live_ranks.shape, jnp.int32),
            pltpu.SMEM(owner_group.shape, jnp.int32),
            pltpu.SMEM(row_counts.shape, jnp.int32),
            pltpu.SMEM(row_offsets.shape, jnp.int32),
            dma((6,)),
        ],
        compiler_params=pltpu.CompilerParams(
            collective_id=0, has_side_effects=True, vmem_limit_bytes=VMEM_LIMIT
        ),
        name="muon_exchange",
    )(*[pltpu.with_memory_space_constraint(each, pltpu.HBM) for each in operands])

    anywhere = pl.BlockSpec(memory_space=pl.ANY)
    flat = (1, columns, INNER)
    new_momentum, update_shards, owned = pl.pallas_call(
        functools.partial(finish_kernel, ranks, columns),
        out_shape=(
            jax.ShapeDtypeStruct(momentum.shape, F32),
            jax.ShapeDtypeStruct(momentum.shape, F32),
            jax.ShapeDtypeStruct(flat, F32),
        ),
        in_specs=[vmem, vmem, vmem, hbm],
        out_specs=(anywhere, anywhere, anywhere),
        scratch_shapes=[
            pltpu.VMEM(momentum.shape, F32),
            pltpu.VMEM(flat, F32),
            pltpu.SMEM(owner_group.shape, jnp.int32),
            dma((5,)),
        ],
        compiler_params=pltpu.CompilerParams(vmem_limit_bytes=VMEM_LIMIT),
        name="muon_finish",
    )(home, result, fresh, pltpu.with_memory_space_constraint(owner_group, pltpu.HBM))
    return (new_momentum, update_shards, jnp.swapaxes(owned, 1, 2))


def solution(mesh, grid=GRID):
    placed = (P(None, "fsdp", "tensor"), P(None, "fsdp", "tensor"), P(), P(), P(), P())
    return jax.shard_map(
        functools.partial(on_device, mesh.shape["fsdp"], grid),
        mesh=mesh,
        in_specs=placed,
        out_specs=(P(None, "fsdp", "tensor"), P(None, "fsdp", "tensor"), P("fsdp", None, "tensor")),
        check_vma=False,
    )
```

```python
import functools
import math

import jax
import jax.numpy as jnp
from jax import lax
from jax.experimental import pallas as pl
from jax.experimental.pallas import tpu as pltpu
from jax.sharding import PartitionSpec as P

WIDTH = 7168
INNER = 576
PADDED = 640
BLOCK = 64
LANES = 128

MOMENTUM_RATE = 0.95
QUINTIC_FIRST = 3.4445
QUINTIC_SECOND = -4.775
QUINTIC_THIRD = 2.0315
EPSILON = 1e-07
SCALE = 0.2 * math.sqrt(max(INNER, WIDTH))

STAGES = 4
GROUPS = (0, 2, 1, 3)
BACK_ORDER = tuple(range(16))
VMEM_LIMIT = 32 * 1024 * 1024

MESH = pl.DeviceIdType.MESH
F32 = jnp.float32
BF16 = jnp.bfloat16

GRID = (8, 4, 2)


def dot(left, right):
    return jnp.dot(left, right, preferred_element_type=F32)


def iota(shape, axis):
    return lax.broadcasted_iota(jnp.int32, shape, axis)


def split(value):
    high = value.astype(BF16)
    low = (value - high.astype(F32)).astype(BF16)
    return high, low


def pack_slots(block):
    rows, columns = block.shape
    spare = LANES - columns
    wide = jnp.concatenate([block, jnp.zeros((rows, spare), F32)], axis=1)
    last = wide[rows - 8 :]
    pieces = []
    for tile in range((rows - 8) // 8):
        if tile * spare < columns:
            pieces.append(pltpu.roll(last, (columns - spare * tile) % LANES, 1))
        else:
            pieces.append(jnp.zeros((8, LANES), F32))
    tail = jnp.concatenate(pieces, axis=0)
    return jnp.where(iota(tail.shape, 1) < columns, wide[: rows - 8], tail)


def unpack_slots(packed, columns):
    spare = LANES - columns
    lane = iota((8, LANES), 1)
    last = jnp.zeros((8, LANES), F32)
    for tile in range(-(-columns // spare)):
        piece = pltpu.roll(packed[8 * tile : 8 * tile + 8], (spare * tile - columns) % LANES, 1)
        last = jnp.where((lane >= spare * tile) & (lane < spare * (tile + 1)), piece, last)
    main = jnp.where(iota(packed.shape, 1) < columns, packed, 0.0)
    return jnp.concatenate([main, last], axis=0)


def pack_gram(gram, store):
    lane = iota((BLOCK, LANES), 1)

    def tile(row, column):
        return gram[BLOCK * row : BLOCK * row + BLOCK, LANES * column : LANES * column + LANES]

    entry = 0
    for p in range(4):
        for column in range(p, 4):
            store(entry, tile(2 * p, column))
            entry += 1
        for column in range(p + 1, 4):
            store(entry, tile(2 * p + 1, column))
            entry += 1
        store(entry, jnp.where(lane < BLOCK, tile(2 * p, 4), tile(2 * p + 1, p)))
        entry += 1
    for row in (1, 5):
        store(entry, jnp.where(lane < BLOCK, tile(row, 4), pltpu.roll(tile(row + 2, 4), BLOCK, 1)))
        entry += 1
    store(entry, tile(8, 4))


ENTRIES = 23


def gram_entries():
    full, merged, entry = {}, {}, 0
    for p in range(4):
        for column in range(p, 4):
            full[2 * p, column] = entry
            entry += 1
        for column in range(p + 1, 4):
            full[2 * p + 1, column] = entry
            entry += 1
        merged[p] = entry
        entry += 1
    return full, merged, {1: entry, 5: entry + 1}, entry + 2


def gram_trace(load):
    full, merged, _, last = gram_entries()
    row, lane = iota((BLOCK, LANES), 0), iota((BLOCK, LANES), 1)
    diagonal = row == lane
    total = jnp.where(diagonal, load(last), 0.0)
    for p in range(4):
        total += jnp.where(diagonal, load(full[2 * p, p]), 0.0)
        total += jnp.where(row + BLOCK == lane, load(merged[p]), 0.0)
    return jnp.sum(total, axis=(0, 1), keepdims=True)


def unpack_gram(load, store):
    full, merged, edge, last = gram_entries()
    half = iota((BLOCK, LANES), 1) < BLOCK
    row, lane = iota((LANES, LANES), 0), iota((LANES, LANES), 1)
    for p in range(4):
        block = jnp.concatenate(
            [load(full[2 * p, p]), jnp.where(half, 0.0, load(merged[p]))], axis=0
        )
        store(p, p, jnp.where((row >= BLOCK) & (lane < BLOCK), block.T, block))
        for q in range(p + 1, 4):
            block = jnp.concatenate([load(full[2 * p, q]), load(full[2 * p + 1, q])], axis=0)
            store(p, q, block)
            store(q, p, block.T)
        odd = 2 * p + 1
        if odd in edge:
            right = load(edge[odd])
        else:
            right = pltpu.roll(load(edge[odd - 2]), BLOCK, 1)
        block = jnp.concatenate(
            [jnp.where(half, load(merged[p]), 0.0), jnp.where(half, right, 0.0)], axis=0
        )
        store(p, 4, block)
        store(4, p, block.T[:BLOCK])
    store(4, 4, jnp.where(half, load(last), 0.0))


def near_first(count):
    order = [0]
    for distance in range(1, count // 2 + 1):
        order.append(distance)
        if distance != count - distance:
            order.append(count - distance)
    return order


def step_kernel(
    ranks,
    grid,
    momentum_out,
    gradient_out,
    live_out,
    owners_out,
    counts_out,
    offsets_out,
    home,
    result,
    fresh,
    sent_in,
    came_in,
    sent_out,
    gathered,
    gram,
    part,
    other,
    row_sum,
    row_in,
    cell_sum,
    cell_in,
    whole,
    halves,
    column,
    kept,
    summed,
    in_send,
    in_recv,
    out_send,
    out_recv,
    core_send,
    core_recv,
    x_send,
    x_recv,
    y_send,
    y_recv,
    momentum,
    gradient,
    live,
    owners,
    counts,
    offsets,
    loads,
):
    y_count, x_count, core_count = grid
    matrices, slots, columns = momentum.shape
    me = lax.axis_index("fsdp")
    here = lax.axis_index("tensor")
    core = lax.rem(here, core_count)
    x_here = lax.rem(here // core_count, x_count)
    y_here = here // (core_count * x_count)

    def rank_at(distance):
        return {"fsdp": lax.rem(me + distance, ranks), "tensor": here}

    def cell(y, x, c):
        return {"fsdp": me, "tensor": (y * x_count + x) * core_count + c}

    sibling = cell(y_here, x_here, 1 - core)
    x_peers = [cell(y_here, lax.rem(x_here + d, x_count), core) for d in range(1, x_count)]
    y_peers = [cell(lax.rem(y_here + d, y_count), x_here, core) for d in range(1, y_count)]

    barrier = pltpu.get_barrier_semaphore()
    peers = [rank_at(d) for d in range(1, ranks)] + [sibling] + x_peers + y_peers
    for peer in peers:
        pl.semaphore_signal(barrier, inc=1, device_id=peer, device_id_type=MESH)

    inputs = (
        (live_out, live),
        (owners_out, owners),
        (counts_out, counts),
        (offsets_out, offsets),
        (momentum_out, momentum),
        (gradient_out, gradient),
    )
    loading = [
        pltpu.make_async_copy(source, target, loads.at[n])
        for n, (source, target) in enumerate(inputs)
    ]
    for load in loading:
        load.start()
    for load in loading:
        load.wait()

    def owned_by(rank):
        found = jnp.int32(0)
        for k in range(matrices):
            found = jnp.where(owners[k] == rank, k, found)
        return found

    mine = owned_by(me)
    for d in range(ranks):
        k = mine if d == 0 else owned_by(lax.rem(me + d, ranks))
        grad = gradient[k]
        blended = grad + MOMENTUM_RATE * (MOMENTUM_RATE * momentum[k] + grad)
        if d == 0:
            came_in[0] = pack_slots(blended)
        else:
            sent_in[d] = pack_slots(blended)

    pl.semaphore_wait(barrier, len(peers))

    def copy_in(d):
        return pltpu.make_async_remote_copy(
            src_ref=sent_in.at[d],
            dst_ref=came_in.at[d],
            send_sem=in_send.at[d],
            recv_sem=in_recv.at[d],
            device_id=rank_at(d),
            device_id_type=MESH,
        )

    order = near_first(ranks)
    copies_in = {d: copy_in(d) for d in range(1, ranks)}
    stride = STAGES
    strands = ranks // stride
    far = sorted(range(strands), key=lambda i: -min(i * stride + 1, ranks - i * stride - 1))
    for group in GROUPS:
        nearest = lax.rem(group + ranks - me, stride)
        for i in far:
            d = nearest + stride * i
            if i == 0:

                @pl.when(d > 0)
                def _():
                    copy_in(d).start()

            else:
                copy_in(d).start()

    rows = iota((slots, columns), 0)
    for k in range(matrices):
        updated = MOMENTUM_RATE * momentum[k] + gradient[k]
        fresh[k] = jnp.where(rows < counts[k, me] * live[me], updated, 0.0)

    def held(rank):
        return offsets[mine, rank], counts[mine, rank] * live[rank]

    for pair in range(ranks // 2):
        blocks, tables = [], []
        for rank in (2 * pair, 2 * pair + 1):
            d = lax.rem(me + ranks - rank, ranks)

            @pl.when(d > 0)
            def _():
                copy_in(d).wait_recv()

            blocks.append(unpack_slots(came_in[d], columns))
            tables.append(held(rank))
        data = jnp.concatenate(split(jnp.concatenate(blocks, axis=0)), axis=1)
        lane = iota((INNER, 2 * slots), 1)
        first = lane < slots
        slot = jnp.where(first, lane, lane - slots)
        offset = jnp.where(first, tables[0][0], tables[1][0])
        count = jnp.where(first, tables[0][1], tables[1][1])
        select = (iota((INNER, 2 * slots), 0) - slot == offset) & (slot < count)
        added = dot(jnp.where(select, 1.0, 0.0).astype(BF16), data)
        if pair == 0:
            gathered[...] = added
        else:
            gathered[...] += added

    both = gathered[...].astype(BF16)
    high, low = both[:, :LANES], both[:, LANES:]
    pad = jnp.zeros((PADDED - INNER, 4 * LANES), BF16)
    left = jnp.concatenate([both, both], axis=1)
    right = jnp.concatenate([jnp.concatenate([high, high, low, low], axis=1), pad], axis=0)
    across = (((1,), (1,)), ((), ()))
    cut = 2 * LANES
    gram[:cut, :] = lax.dot_general(left[:cut], right, across, preferred_element_type=F32)
    gram[cut:, cut:] = lax.dot_general(left[cut:], right[cut:], across, preferred_element_type=F32)

    def put(entry, tile):
        part[BLOCK * entry : BLOCK * entry + BLOCK, :] = tile

    pack_gram(gram, put)
    total_rows = part.shape[0]
    if total_rows > BLOCK * ENTRIES:
        part[BLOCK * ENTRIES :, :] = jnp.zeros((total_rows - BLOCK * ENTRIES, LANES), F32)

    piece = total_rows // (core_count * y_count * x_count)

    def place(ref, index, count=1):
        size = piece * count
        return ref.at[pl.ds(pl.multiple_of(index * piece, 8), size), :]

    pending = []

    def send(src, dst, peer, send_sem, recv_sem):
        copy = pltpu.make_async_remote_copy(
            src_ref=src,
            dst_ref=dst,
            send_sem=send_sem,
            recv_sem=recv_sem,
            device_id=peer,
            device_id_type=MESH,
        )
        copy.start()
        pending.append(copy)
        return copy

    cells = y_count * x_count
    y_order = near_first(y_count)
    x_order = near_first(x_count)[1:]

    def y_at(d):
        return lax.rem(y_here + d, y_count)

    def x_at(d):
        return lax.rem(x_here + d, x_count)

    copies = {}
    for d in y_order[::-1]:
        line = y_at(d) * x_count
        copies[d] = send(
            place(part, (1 - core) * cells + line, x_count),
            place(other, line, x_count),
            sibling,
            core_send.at[d],
            core_recv.at[d],
        )
    x_copies = {}
    for d in y_order[::-1]:
        line = y_at(d) * x_count
        copies[d].wait_recv()
        place(row_sum, line, x_count)[...] = (
            place(part, core * cells + line, x_count)[...] + place(other, line, x_count)[...]
        )
        for e in x_order[::-1]:
            slot = d * x_count + e
            x_copies[d, e] = send(
                place(row_sum, line + x_at(e)),
                row_in.at[slot],
                x_peers[e - 1],
                x_send.at[slot],
                x_recv.at[slot],
            )
    y_copies = {}
    for d in y_order[::-1]:
        total = place(row_sum, y_at(d) * x_count + x_here)[...]
        for e in x_order:
            x_copies[d, e].wait_recv()
            total = total + row_in[d * x_count + e]
        if d == 0:
            own_total = total
        else:
            cell_sum[d] = total
            y_copies[d] = send(
                cell_sum.at[d], cell_in.at[d], y_peers[d - 1], y_send.at[d], y_recv.at[d]
            )
    total = own_total
    for d in y_order[1:]:
        y_copies[d].wait_recv()
        total = total + cell_in[d]

    def home_of(d, e):
        return place(whole, core * cells + y_at(d) * x_count + x_at(e))

    home_of(0, 0)[...] = total
    for d in y_order[:0:-1]:
        y_copies[d] = send(
            home_of(0, 0),
            home_of(0, 0),
            y_peers[d - 1],
            y_send.at[y_count + d],
            y_recv.at[y_count + d],
        )
    core_copies = []
    for d in y_order:
        back = lax.rem(y_count - d, y_count)
        if d > 0:
            y_copies[d].wait_recv()
        for e in x_order[::-1]:
            slot = (y_count + d) * x_count + e
            x_copies[d, e] = send(
                home_of(back, 0),
                home_of(back, 0),
                x_peers[e - 1],
                x_send.at[slot],
                x_recv.at[slot],
            )
    for d in y_order:
        back = lax.rem(y_count - d, y_count)
        for e in x_order:
            x_copies[d, e].wait_recv()
        line = place(whole, core * cells + y_at(back) * x_count, x_count)
        slot = y_count + d
        core_copies.append(send(line, line, sibling, core_send.at[slot], core_recv.at[slot]))
    for copy in core_copies:
        copy.wait_recv()

    def load(entry):
        return whole[BLOCK * entry : BLOCK * entry + BLOCK, :]

    inverse = 1.0 / (jnp.sqrt(gram_trace(load)) + EPSILON)

    def keep(p, q, block):
        high, low = split((block * inverse) * inverse)
        rows, lanes = slice(LANES * p, LANES * p + block.shape[0]), LANES * q
        halves[rows, lanes : lanes + LANES] = high
        halves[rows, PADDED + lanes : PADDED + lanes + LANES] = low

    unpack_gram(load, keep)

    for base in (0, PADDED):
        column[base + INNER : base + PADDED, :] = jnp.zeros((PADDED - INNER, 2 * LANES), BF16)

    def stack(value):
        both = jnp.concatenate(split(value), axis=1)
        column[:INNER, :] = both
        column[PADDED : PADDED + INNER, :] = both

    start = (gathered[:, :LANES] + gathered[:, LANES:]) * inverse
    kept[...] = start
    summed[...] = jnp.zeros_like(start)
    stack(start)

    @pl.loop(0, 12)
    def _(index):
        phase = lax.rem(index + 3, 5)
        opens = (phase == 3) | (phase == 1)
        closes = (phase == 4) | (phase == 2)
        keep_part = jnp.where(opens, QUINTIC_SECOND, jnp.where(closes, QUINTIC_FIRST, 0.0))
        product_part = jnp.where(opens, QUINTIC_THIRD, 1.0)
        sum_part = jnp.where(
            index == 1,
            QUINTIC_FIRST,
            jnp.where(index == 6, QUINTIC_SECOND, jnp.where(index == 11, QUINTIC_THIRD, 0.0)),
        )
        product = dot(halves[...], column[...])
        value = keep_part * kept[...] + product_part * (product[:, :LANES] + product[:, LANES:])
        stack(value)
        kept[...] = jnp.where(opens, kept[...], value)
        summed[...] += sum_part * value

    final = summed[...] * SCALE
    result[...] = final
    stack(final)
    sent = column[:PADDED, :]
    def copy_out(rank, d):
        return pltpu.make_async_remote_copy(
            src_ref=sent_out.at[rank],
            dst_ref=home.at[d],
            send_sem=out_send.at[d],
            recv_sem=out_recv.at[d],
            device_id={"fsdp": rank, "tensor": here},
            device_id_type=MESH,
        )

    for pair in range(ranks // 2):
        targets = BACK_ORDER[2 * pair : 2 * pair + 2] if ranks == 16 else (2 * pair, 2 * pair + 1)
        tables = [held(rank) for rank in targets]
        row = iota((2 * slots, PADDED), 0)
        first = row < slots
        slot = jnp.where(first, row, row - slots)
        offset = jnp.where(first, tables[0][0], tables[1][0])
        count = jnp.where(first, tables[0][1], tables[1][1])
        select = (iota((2 * slots, PADDED), 1) - slot == offset) & (slot < count)
        picked = dot(jnp.where(select, 1.0, 0.0).astype(BF16), sent)
        picked = (picked[:, :LANES] + picked[:, LANES:])[:, :columns]
        for place, rank in enumerate(targets):
            d = lax.rem(rank + ranks - me, ranks)
            sent_out[rank] = pack_slots(picked[place * slots : place * slots + slots])

            @pl.when(d == 0)
            def _():
                home[0] = sent_out[rank]

            @pl.when(d > 0)
            def _():
                copy_out(rank, d).start()

    copies_out = [copy_out(lax.rem(me + d, ranks), d) for d in range(1, ranks)]
    for copy in copies_out:
        copy.wait_recv()
    for copy in list(copies_in.values()) + pending + copies_out:
        copy.wait_send()


def finish_kernel(
    ranks,
    columns,
    home,
    result,
    fresh,
    owners_out,
    new_momentum,
    update,
    owned,
    update_here,
    owned_here,
    owners,
    sems,
):
    me = lax.axis_index("fsdp")
    load = pltpu.make_async_copy(owners_out, owners, sems.at[4])
    load.start()
    copies = [pltpu.make_async_copy(fresh, new_momentum, sems.at[0])]
    copies[0].start()
    owned_here[0] = result[...].T[:columns]
    copies.append(pltpu.make_async_copy(owned_here, owned, sems.at[1]))
    copies[1].start()
    load.wait()
    half = update.shape[0] // 2
    for k in range(update.shape[0]):
        source = lax.rem(me + ranks - owners[k], ranks)
        update_here[k] = unpack_slots(home[source], columns)[:, :columns]
        if k + 1 in (half, 2 * half):
            part = pl.ds(k + 1 - half, half)
            copies.append(
                pltpu.make_async_copy(
                    update_here.at[part], update.at[part], sems.at[2 + k // half]
                )
            )
            copies[-1].start()
    for copy in copies:
        copy.wait()


def on_device(ranks, grid, momentum, gradient, live_ranks, owner_group, row_counts, row_offsets):
    y_count, x_count, core_count = grid
    matrices, slots, columns = momentum.shape
    cells = y_count * x_count * core_count
    piece = -(-8 * ENTRIES // cells) * 8
    total_rows = piece * cells
    half_rows = total_rows // core_count

    vmem = pl.BlockSpec(memory_space=pltpu.VMEM)
    hbm = pl.BlockSpec(memory_space=pltpu.HBM)
    packed = (ranks, slots - 8, LANES)
    dma = pltpu.SemaphoreType.DMA
    operands = (momentum, gradient, live_ranks, owner_group, row_counts, row_offsets)
    home, result, fresh = pl.pallas_call(
        functools.partial(step_kernel, ranks, grid),
        out_shape=(
            jax.ShapeDtypeStruct(packed, F32),
            jax.ShapeDtypeStruct((INNER, LANES), F32),
            jax.ShapeDtypeStruct(momentum.shape, F32),
        ),
        in_specs=[hbm] * 6,
        out_specs=(vmem, vmem, vmem),
        scratch_shapes=[
            pltpu.VMEM(packed, F32),
            pltpu.VMEM(packed, F32),
            pltpu.VMEM(packed, F32),
            pltpu.VMEM((INNER, 2 * LANES), F32),
            pltpu.VMEM((INNER, PADDED), F32),
            pltpu.VMEM((total_rows, LANES), F32),
            pltpu.VMEM((half_rows, LANES), F32),
            pltpu.VMEM((half_rows, LANES), F32),
            pltpu.VMEM((y_count * x_count, piece, LANES), F32),
            pltpu.VMEM((y_count, piece, LANES), F32),
            pltpu.VMEM((y_count, piece, LANES), F32),
            pltpu.VMEM((total_rows, LANES), F32),
            pltpu.VMEM((INNER, 2 * PADDED), BF16),
            pltpu.VMEM((2 * PADDED, 2 * LANES), BF16),
            pltpu.VMEM((INNER, LANES), F32),
            pltpu.VMEM((INNER, LANES), F32),
            dma((ranks,)),
            dma((ranks,)),
            dma((ranks,)),
            dma((ranks,)),
            dma((y_count * (1 + x_count),)),
            dma((y_count * (1 + x_count),)),
            dma((2 * y_count * x_count,)),
            dma((2 * y_count * x_count,)),
            dma((2 * y_count,)),
            dma((2 * y_count,)),
            pltpu.VMEM(momentum.shape, F32),
            pltpu.VMEM(gradient.shape, F32),
            pltpu.SMEM(live_ranks.shape, jnp.int32),
            pltpu.SMEM(owner_group.shape, jnp.int32),
            pltpu.SMEM(row_counts.shape, jnp.int32),
            pltpu.SMEM(row_offsets.shape, jnp.int32),
            dma((6,)),
        ],
        compiler_params=pltpu.CompilerParams(
            collective_id=0, has_side_effects=True, vmem_limit_bytes=VMEM_LIMIT
        ),
        name="muon_exchange",
    )(*[pltpu.with_memory_space_constraint(each, pltpu.HBM) for each in operands])

    anywhere = pl.BlockSpec(memory_space=pl.ANY)
    flat = (1, columns, INNER)
    new_momentum, update_shards, owned = pl.pallas_call(
        functools.partial(finish_kernel, ranks, columns),
        out_shape=(
            jax.ShapeDtypeStruct(momentum.shape, F32),
            jax.ShapeDtypeStruct(momentum.shape, F32),
            jax.ShapeDtypeStruct(flat, F32),
        ),
        in_specs=[vmem, vmem, vmem, hbm],
        out_specs=(anywhere, anywhere, anywhere),
        scratch_shapes=[
            pltpu.VMEM(momentum.shape, F32),
            pltpu.VMEM(flat, F32),
            pltpu.SMEM(owner_group.shape, jnp.int32),
            dma((5,)),
        ],
        compiler_params=pltpu.CompilerParams(vmem_limit_bytes=VMEM_LIMIT),
        name="muon_finish",
    )(home, result, fresh, pltpu.with_memory_space_constraint(owner_group, pltpu.HBM))
    return (new_momentum, update_shards, jnp.swapaxes(owned, 1, 2))


def solution(mesh, grid=GRID):
    placed = (P(None, "fsdp", "tensor"), P(None, "fsdp", "tensor"), P(), P(), P(), P())
    return jax.shard_map(
        functools.partial(on_device, mesh.shape["fsdp"], grid),
        mesh=mesh,
        in_specs=placed,
        out_specs=(P(None, "fsdp", "tensor"), P(None, "fsdp", "tensor"), P("fsdp", None, "tensor")),
        check_vma=False,
    )
```

```python
import functools
import math

import jax
import jax.numpy as jnp
from jax import lax
from jax.experimental import pallas as pl
from jax.experimental.pallas import tpu as pltpu
from jax.sharding import PartitionSpec as P

WIDTH = 7168
INNER = 576
PADDED = 640
BLOCK = 64
LANES = 128

MOMENTUM_RATE = 0.95
QUINTIC_FIRST = 3.4445
QUINTIC_SECOND = -4.775
QUINTIC_THIRD = 2.0315
EPSILON = 1e-07
SCALE = 0.2 * math.sqrt(max(INNER, WIDTH))

STAGES = 4
GROUPS = (0, 2, 1, 3)
BACK_ORDER = tuple(range(16))
VMEM_LIMIT = 32 * 1024 * 1024

MESH = pl.DeviceIdType.MESH
F32 = jnp.float32
BF16 = jnp.bfloat16

GRID = (8, 4, 2)


def dot(left, right):
    return jnp.dot(left, right, preferred_element_type=F32)


def iota(shape, axis):
    return lax.broadcasted_iota(jnp.int32, shape, axis)


def split(value):
    high = value.astype(BF16)
    low = (value - high.astype(F32)).astype(BF16)
    return high, low


def pack_slots(block):
    rows, columns = block.shape
    spare = LANES - columns
    wide = jnp.concatenate([block, jnp.zeros((rows, spare), F32)], axis=1)
    last = wide[rows - 8 :]
    pieces = []
    for tile in range((rows - 8) // 8):
        if tile * spare < columns:
            pieces.append(pltpu.roll(last, (columns - spare * tile) % LANES, 1))
        else:
            pieces.append(jnp.zeros((8, LANES), F32))
    tail = jnp.concatenate(pieces, axis=0)
    return jnp.where(iota(tail.shape, 1) < columns, wide[: rows - 8], tail)


def unpack_slots(packed, columns):
    spare = LANES - columns
    lane = iota((8, LANES), 1)
    last = jnp.zeros((8, LANES), F32)
    for tile in range(-(-columns // spare)):
        piece = pltpu.roll(packed[8 * tile : 8 * tile + 8], (spare * tile - columns) % LANES, 1)
        last = jnp.where((lane >= spare * tile) & (lane < spare * (tile + 1)), piece, last)
    main = jnp.where(iota(packed.shape, 1) < columns, packed, 0.0)
    return jnp.concatenate([main, last], axis=0)


def pack_gram(gram, store):
    lane = iota((BLOCK, LANES), 1)

    def tile(row, column):
        return gram[BLOCK * row : BLOCK * row + BLOCK, LANES * column : LANES * column + LANES]

    entry = 0
    for p in range(4):
        for column in range(p, 4):
            store(entry, tile(2 * p, column))
            entry += 1
        for column in range(p + 1, 4):
            store(entry, tile(2 * p + 1, column))
            entry += 1
        store(entry, jnp.where(lane < BLOCK, tile(2 * p, 4), tile(2 * p + 1, p)))
        entry += 1
    for row in (1, 5):
        store(entry, jnp.where(lane < BLOCK, tile(row, 4), pltpu.roll(tile(row + 2, 4), BLOCK, 1)))
        entry += 1
    store(entry, tile(8, 4))


ENTRIES = 23


def gram_entries():
    full, merged, entry = {}, {}, 0
    for p in range(4):
        for column in range(p, 4):
            full[2 * p, column] = entry
            entry += 1
        for column in range(p + 1, 4):
            full[2 * p + 1, column] = entry
            entry += 1
        merged[p] = entry
        entry += 1
    return full, merged, {1: entry, 5: entry + 1}, entry + 2


def gram_trace(load):
    full, merged, _, last = gram_entries()
    row, lane = iota((BLOCK, LANES), 0), iota((BLOCK, LANES), 1)
    diagonal = row == lane
    total = jnp.where(diagonal, load(last), 0.0)
    for p in range(4):
        total += jnp.where(diagonal, load(full[2 * p, p]), 0.0)
        total += jnp.where(row + BLOCK == lane, load(merged[p]), 0.0)
    return jnp.sum(total, axis=(0, 1), keepdims=True)


def unpack_gram(load, store):
    full, merged, edge, last = gram_entries()
    half = iota((BLOCK, LANES), 1) < BLOCK
    row, lane = iota((LANES, LANES), 0), iota((LANES, LANES), 1)
    for p in range(4):
        block = jnp.concatenate(
            [load(full[2 * p, p]), jnp.where(half, 0.0, load(merged[p]))], axis=0
        )
        store(p, p, jnp.where((row >= BLOCK) & (lane < BLOCK), block.T, block))
        for q in range(p + 1, 4):
            block = jnp.concatenate([load(full[2 * p, q]), load(full[2 * p + 1, q])], axis=0)
            store(p, q, block)
            store(q, p, block.T)
        odd = 2 * p + 1
        if odd in edge:
            right = load(edge[odd])
        else:
            right = pltpu.roll(load(edge[odd - 2]), BLOCK, 1)
        block = jnp.concatenate(
            [jnp.where(half, load(merged[p]), 0.0), jnp.where(half, right, 0.0)], axis=0
        )
        store(p, 4, block)
        store(4, p, block.T[:BLOCK])
    store(4, 4, jnp.where(half, load(last), 0.0))


def near_first(count):
    order = [0]
    for distance in range(1, count // 2 + 1):
        order.append(distance)
        if distance != count - distance:
            order.append(count - distance)
    return order


def step_kernel(
    ranks,
    grid,
    momentum_out,
    gradient_out,
    live_out,
    owners_out,
    counts_out,
    offsets_out,
    home,
    result,
    fresh,
    sent_in,
    came_in,
    sent_out,
    gathered,
    gram,
    part,
    other,
    row_sum,
    row_in,
    cell_sum,
    cell_in,
    whole,
    halves,
    column,
    kept,
    summed,
    in_send,
    in_recv,
    out_send,
    out_recv,
    core_send,
    core_recv,
    x_send,
    x_recv,
    y_send,
    y_recv,
    momentum,
    gradient,
    live,
    owners,
    counts,
    offsets,
    loads,
):
    y_count, x_count, core_count = grid
    matrices, slots, columns = momentum.shape
    me = lax.axis_index("fsdp")
    here = lax.axis_index("tensor")
    core = lax.rem(here, core_count)
    x_here = lax.rem(here // core_count, x_count)
    y_here = here // (core_count * x_count)

    def rank_at(distance):
        return {"fsdp": lax.rem(me + distance, ranks), "tensor": here}

    def cell(y, x, c):
        return {"fsdp": me, "tensor": (y * x_count + x) * core_count + c}

    sibling = cell(y_here, x_here, 1 - core)
    x_peers = [cell(y_here, lax.rem(x_here + d, x_count), core) for d in range(1, x_count)]
    y_peers = [cell(lax.rem(y_here + d, y_count), x_here, core) for d in range(1, y_count)]

    barrier = pltpu.get_barrier_semaphore()
    peers = [rank_at(d) for d in range(1, ranks)] + [sibling] + x_peers + y_peers
    for peer in peers:
        pl.semaphore_signal(barrier, inc=1, device_id=peer, device_id_type=MESH)

    inputs = (
        (live_out, live),
        (owners_out, owners),
        (counts_out, counts),
        (offsets_out, offsets),
        (momentum_out, momentum),
        (gradient_out, gradient),
    )
    loading = [
        pltpu.make_async_copy(source, target, loads.at[n])
        for n, (source, target) in enumerate(inputs)
    ]
    for load in loading:
        load.start()
    for load in loading:
        load.wait()

    def owned_by(rank):
        found = jnp.int32(0)
        for k in range(matrices):
            found = jnp.where(owners[k] == rank, k, found)
        return found

    mine = owned_by(me)
    for d in range(ranks):
        k = mine if d == 0 else owned_by(lax.rem(me + d, ranks))
        grad = gradient[k]
        blended = grad + MOMENTUM_RATE * (MOMENTUM_RATE * momentum[k] + grad)
        if d == 0:
            came_in[0] = pack_slots(blended)
        else:
            sent_in[d] = pack_slots(blended)

    pl.semaphore_wait(barrier, len(peers))

    def copy_in(d):
        return pltpu.make_async_remote_copy(
            src_ref=sent_in.at[d],
            dst_ref=came_in.at[d],
            send_sem=in_send.at[d],
            recv_sem=in_recv.at[d],
            device_id=rank_at(d),
            device_id_type=MESH,
        )

    order = near_first(ranks)
    copies_in = {d: copy_in(d) for d in range(1, ranks)}
    stride = STAGES
    strands = ranks // stride
    far = sorted(range(strands), key=lambda i: -min(i * stride + 1, ranks - i * stride - 1))
    for group in GROUPS:
        nearest = lax.rem(group + ranks - me, stride)
        for i in far:
            d = nearest + stride * i
            if i == 0:

                @pl.when(d > 0)
                def _():
                    copy_in(d).start()

            else:
                copy_in(d).start()

    rows = iota((slots, columns), 0)
    for k in range(matrices):
        updated = MOMENTUM_RATE * momentum[k] + gradient[k]
        fresh[k] = jnp.where(rows < counts[k, me] * live[me], updated, 0.0)

    def held(rank):
        return offsets[mine, rank], counts[mine, rank] * live[rank]

    for pair in range(ranks // 2):
        blocks, tables = [], []
        for rank in (2 * pair, 2 * pair + 1):
            d = lax.rem(me + ranks - rank, ranks)

            @pl.when(d > 0)
            def _():
                copy_in(d).wait_recv()

            blocks.append(unpack_slots(came_in[d], columns))
            tables.append(held(rank))
        data = jnp.concatenate(split(jnp.concatenate(blocks, axis=0)), axis=1)
        lane = iota((INNER, 2 * slots), 1)
        first = lane < slots
        slot = jnp.where(first, lane, lane - slots)
        offset = jnp.where(first, tables[0][0], tables[1][0])
        count = jnp.where(first, tables[0][1], tables[1][1])
        select = (iota((INNER, 2 * slots), 0) - slot == offset) & (slot < count)
        added = dot(jnp.where(select, 1.0, 0.0).astype(BF16), data)
        if pair == 0:
            gathered[...] = added
        else:
            gathered[...] += added

    both = gathered[...].astype(BF16)
    high, low = both[:, :LANES], both[:, LANES:]
    pad = jnp.zeros((PADDED - INNER, 4 * LANES), BF16)
    left = jnp.concatenate([both, both], axis=1)
    right = jnp.concatenate([jnp.concatenate([high, high, low, low], axis=1), pad], axis=0)
    across = (((1,), (1,)), ((), ()))
    cut = 2 * LANES
    gram[:cut, :] = lax.dot_general(left[:cut], right, across, preferred_element_type=F32)
    gram[cut:, cut:] = lax.dot_general(left[cut:], right[cut:], across, preferred_element_type=F32)

    def put(entry, tile):
        part[BLOCK * entry : BLOCK * entry + BLOCK, :] = tile

    pack_gram(gram, put)
    total_rows = part.shape[0]
    if total_rows > BLOCK * ENTRIES:
        part[BLOCK * ENTRIES :, :] = jnp.zeros((total_rows - BLOCK * ENTRIES, LANES), F32)

    piece = total_rows // (core_count * y_count * x_count)

    def place(ref, index, count=1):
        size = piece * count
        return ref.at[pl.ds(pl.multiple_of(index * piece, 8), size), :]

    pending = []

    def send(src, dst, peer, send_sem, recv_sem):
        copy = pltpu.make_async_remote_copy(
            src_ref=src,
            dst_ref=dst,
            send_sem=send_sem,
            recv_sem=recv_sem,
            device_id=peer,
            device_id_type=MESH,
        )
        copy.start()
        pending.append(copy)
        return copy

    cells = y_count * x_count
    y_order = near_first(y_count)
    x_order = near_first(x_count)[1:]

    def y_at(d):
        return lax.rem(y_here + d, y_count)

    def x_at(d):
        return lax.rem(x_here + d, x_count)

    copies = {}
    for d in y_order[::-1]:
        line = y_at(d) * x_count
        copies[d] = send(
            place(part, (1 - core) * cells + line, x_count),
            place(other, line, x_count),
            sibling,
            core_send.at[d],
            core_recv.at[d],
        )
    x_copies = {}
    for d in y_order[::-1]:
        line = y_at(d) * x_count
        copies[d].wait_recv()
        place(row_sum, line, x_count)[...] = (
            place(part, core * cells + line, x_count)[...] + place(other, line, x_count)[...]
        )
        for e in x_order[::-1]:
            slot = d * x_count + e
            x_copies[d, e] = send(
                place(row_sum, line + x_at(e)),
                row_in.at[slot],
                x_peers[e - 1],
                x_send.at[slot],
                x_recv.at[slot],
            )
    y_copies = {}
    for d in y_order[::-1]:
        total = place(row_sum, y_at(d) * x_count + x_here)[...]
        for e in x_order:
            x_copies[d, e].wait_recv()
            total = total + row_in[d * x_count + e]
        if d == 0:
            own_total = total
        else:
            cell_sum[d] = total
            y_copies[d] = send(
                cell_sum.at[d], cell_in.at[d], y_peers[d - 1], y_send.at[d], y_recv.at[d]
            )
    total = own_total
    for d in y_order[1:]:
        y_copies[d].wait_recv()
        total = total + cell_in[d]

    def home_of(d, e):
        return place(whole, core * cells + y_at(d) * x_count + x_at(e))

    home_of(0, 0)[...] = total
    for d in y_order[:0:-1]:
        y_copies[d] = send(
            home_of(0, 0),
            home_of(0, 0),
            y_peers[d - 1],
            y_send.at[y_count + d],
            y_recv.at[y_count + d],
        )
    core_copies = []
    for d in y_order:
        back = lax.rem(y_count - d, y_count)
        if d > 0:
            y_copies[d].wait_recv()
        for e in x_order[::-1]:
            slot = (y_count + d) * x_count + e
            x_copies[d, e] = send(
                home_of(back, 0),
                home_of(back, 0),
                x_peers[e - 1],
                x_send.at[slot],
                x_recv.at[slot],
            )
    for d in y_order:
        back = lax.rem(y_count - d, y_count)
        for e in x_order:
            x_copies[d, e].wait_recv()
        line = place(whole, core * cells + y_at(back) * x_count, x_count)
        slot = y_count + d
        core_copies.append(send(line, line, sibling, core_send.at[slot], core_recv.at[slot]))
    for copy in core_copies:
        copy.wait_recv()

    def load(entry):
        return whole[BLOCK * entry : BLOCK * entry + BLOCK, :]

    inverse = 1.0 / (jnp.sqrt(gram_trace(load)) + EPSILON)

    def keep(p, q, block):
        high, low = split((block * inverse) * inverse)
        rows, lanes = slice(LANES * p, LANES * p + block.shape[0]), LANES * q
        halves[rows, lanes : lanes + LANES] = high
        halves[rows, PADDED + lanes : PADDED + lanes + LANES] = low

    unpack_gram(load, keep)

    for base in (0, PADDED):
        column[base + INNER : base + PADDED, :] = jnp.zeros((PADDED - INNER, 2 * LANES), BF16)

    def stack(value):
        both = jnp.concatenate(split(value), axis=1)
        column[:INNER, :] = both
        column[PADDED : PADDED + INNER, :] = both

    start = (gathered[:, :LANES] + gathered[:, LANES:]) * inverse
    kept[...] = start
    stack(start)

    def product():
        both = dot(halves[...], column[...])
        return both[:, :LANES] + both[:, LANES:]

    def polynomial():
        stack(QUINTIC_SECOND * kept[...] + QUINTIC_THIRD * product())
        return QUINTIC_FIRST * kept[...] + product()

    value = polynomial()
    kept[...] = value
    summed[...] = QUINTIC_FIRST * value
    stack(value)

    @pl.loop(0, 2)
    def _(turn):
        value = product()
        kept[...] = value
        stack(value)
        value = polynomial()
        kept[...] = value
        stack(value)
        value = polynomial()
        stack(value)
        summed[...] += jnp.where(turn == 0, QUINTIC_SECOND, QUINTIC_THIRD) * value

    final = summed[...] * SCALE
    result[...] = final
    stack(final)
    sent = column[:PADDED, :]
    def copy_out(rank, d):
        return pltpu.make_async_remote_copy(
            src_ref=sent_out.at[rank],
            dst_ref=home.at[d],
            send_sem=out_send.at[d],
            recv_sem=out_recv.at[d],
            device_id={"fsdp": rank, "tensor": here},
            device_id_type=MESH,
        )

    for pair in range(ranks // 2):
        targets = BACK_ORDER[2 * pair : 2 * pair + 2] if ranks == 16 else (2 * pair, 2 * pair + 1)
        tables = [held(rank) for rank in targets]
        row = iota((2 * slots, PADDED), 0)
        first = row < slots
        slot = jnp.where(first, row, row - slots)
        offset = jnp.where(first, tables[0][0], tables[1][0])
        count = jnp.where(first, tables[0][1], tables[1][1])
        select = (iota((2 * slots, PADDED), 1) - slot == offset) & (slot < count)
        picked = dot(jnp.where(select, 1.0, 0.0).astype(BF16), sent)
        picked = (picked[:, :LANES] + picked[:, LANES:])[:, :columns]
        for place, rank in enumerate(targets):
            d = lax.rem(rank + ranks - me, ranks)
            sent_out[rank] = pack_slots(picked[place * slots : place * slots + slots])

            @pl.when(d == 0)
            def _():
                home[0] = sent_out[rank]

            @pl.when(d > 0)
            def _():
                copy_out(rank, d).start()

    copies_out = [copy_out(lax.rem(me + d, ranks), d) for d in range(1, ranks)]
    for copy in copies_out:
        copy.wait_recv()
    for copy in list(copies_in.values()) + pending + copies_out:
        copy.wait_send()


def finish_kernel(
    ranks,
    columns,
    home,
    result,
    fresh,
    owners_out,
    new_momentum,
    update,
    owned,
    update_here,
    owned_here,
    owners,
    sems,
):
    me = lax.axis_index("fsdp")
    load = pltpu.make_async_copy(owners_out, owners, sems.at[4])
    load.start()
    copies = [pltpu.make_async_copy(fresh, new_momentum, sems.at[0])]
    copies[0].start()
    owned_here[0] = result[...].T[:columns]
    copies.append(pltpu.make_async_copy(owned_here, owned, sems.at[1]))
    copies[1].start()
    load.wait()
    half = update.shape[0] // 2
    for k in range(update.shape[0]):
        source = lax.rem(me + ranks - owners[k], ranks)
        update_here[k] = unpack_slots(home[source], columns)[:, :columns]
        if k + 1 in (half, 2 * half):
            part = pl.ds(k + 1 - half, half)
            copies.append(
                pltpu.make_async_copy(
                    update_here.at[part], update.at[part], sems.at[2 + k // half]
                )
            )
            copies[-1].start()
    for copy in copies:
        copy.wait()


def on_device(ranks, grid, momentum, gradient, live_ranks, owner_group, row_counts, row_offsets):
    y_count, x_count, core_count = grid
    matrices, slots, columns = momentum.shape
    cells = y_count * x_count * core_count
    piece = -(-8 * ENTRIES // cells) * 8
    total_rows = piece * cells
    half_rows = total_rows // core_count

    vmem = pl.BlockSpec(memory_space=pltpu.VMEM)
    hbm = pl.BlockSpec(memory_space=pltpu.HBM)
    packed = (ranks, slots - 8, LANES)
    dma = pltpu.SemaphoreType.DMA
    operands = (momentum, gradient, live_ranks, owner_group, row_counts, row_offsets)
    home, result, fresh = pl.pallas_call(
        functools.partial(step_kernel, ranks, grid),
        out_shape=(
            jax.ShapeDtypeStruct(packed, F32),
            jax.ShapeDtypeStruct((INNER, LANES), F32),
            jax.ShapeDtypeStruct(momentum.shape, F32),
        ),
        in_specs=[hbm] * 6,
        out_specs=(vmem, vmem, vmem),
        scratch_shapes=[
            pltpu.VMEM(packed, F32),
            pltpu.VMEM(packed, F32),
            pltpu.VMEM(packed, F32),
            pltpu.VMEM((INNER, 2 * LANES), F32),
            pltpu.VMEM((INNER, PADDED), F32),
            pltpu.VMEM((total_rows, LANES), F32),
            pltpu.VMEM((half_rows, LANES), F32),
            pltpu.VMEM((half_rows, LANES), F32),
            pltpu.VMEM((y_count * x_count, piece, LANES), F32),
            pltpu.VMEM((y_count, piece, LANES), F32),
            pltpu.VMEM((y_count, piece, LANES), F32),
            pltpu.VMEM((total_rows, LANES), F32),
            pltpu.VMEM((INNER, 2 * PADDED), BF16),
            pltpu.VMEM((2 * PADDED, 2 * LANES), BF16),
            pltpu.VMEM((INNER, LANES), F32),
            pltpu.VMEM((INNER, LANES), F32),
            dma((ranks,)),
            dma((ranks,)),
            dma((ranks,)),
            dma((ranks,)),
            dma((y_count * (1 + x_count),)),
            dma((y_count * (1 + x_count),)),
            dma((2 * y_count * x_count,)),
            dma((2 * y_count * x_count,)),
            dma((2 * y_count,)),
            dma((2 * y_count,)),
            pltpu.VMEM(momentum.shape, F32),
            pltpu.VMEM(gradient.shape, F32),
            pltpu.SMEM(live_ranks.shape, jnp.int32),
            pltpu.SMEM(owner_group.shape, jnp.int32),
            pltpu.SMEM(row_counts.shape, jnp.int32),
            pltpu.SMEM(row_offsets.shape, jnp.int32),
            dma((6,)),
        ],
        compiler_params=pltpu.CompilerParams(
            collective_id=0, has_side_effects=True, vmem_limit_bytes=VMEM_LIMIT
        ),
        name="muon_exchange",
    )(*[pltpu.with_memory_space_constraint(each, pltpu.HBM) for each in operands])

    anywhere = pl.BlockSpec(memory_space=pl.ANY)
    flat = (1, columns, INNER)
    new_momentum, update_shards, owned = pl.pallas_call(
        functools.partial(finish_kernel, ranks, columns),
        out_shape=(
            jax.ShapeDtypeStruct(momentum.shape, F32),
            jax.ShapeDtypeStruct(momentum.shape, F32),
            jax.ShapeDtypeStruct(flat, F32),
        ),
        in_specs=[vmem, vmem, vmem, hbm],
        out_specs=(anywhere, anywhere, anywhere),
        scratch_shapes=[
            pltpu.VMEM(momentum.shape, F32),
            pltpu.VMEM(flat, F32),
            pltpu.SMEM(owner_group.shape, jnp.int32),
            dma((5,)),
        ],
        compiler_params=pltpu.CompilerParams(vmem_limit_bytes=VMEM_LIMIT),
        name="muon_finish",
    )(home, result, fresh, pltpu.with_memory_space_constraint(owner_group, pltpu.HBM))
    return (new_momentum, update_shards, jnp.swapaxes(owned, 1, 2))


def solution(mesh, grid=GRID):
    placed = (P(None, "fsdp", "tensor"), P(None, "fsdp", "tensor"), P(), P(), P(), P())
    return jax.shard_map(
        functools.partial(on_device, mesh.shape["fsdp"], grid),
        mesh=mesh,
        in_specs=placed,
        out_specs=(P(None, "fsdp", "tensor"), P(None, "fsdp", "tensor"), P("fsdp", None, "tensor")),
        check_vma=False,
    )
```
